256 devices in a mesh: ka: 4 (over y_lo, core), fft: 64 (over z, x, y_hi).
Axes of the slice: x: 4, y: 4 (y_hi: 2, y_lo: 2; y = y_hi * 2 + y_lo), z: 8, core: 2. Of those that a mesh axis runs over, the one named last changes fastest.
Arguments:
- orbitals: float32 [4, 1, 2, 128, 128, 128], P('ka', None, None, 'fft'), may hold values from -3 to 3
- costate: float32 [4, 1, 2, 128, 128, 128], P('ka', None, None, 'fft'), may hold values from -6 to 6
- potential: float32 [128, 128, 128], P('fft'), may hold values from -4 to 4
- xc_kernel: float32 [128, 128, 128], P('fft'), may hold values from -1 to -0.1
- vector_potential: float32 [8], replicated, may hold values from -0.6 to 0.6
- kpoint_weight: int32 [4], replicated, may hold values from 1 to 8
- occupation: int32 [1], replicated, may hold values from 100 to 200
Outputs:
- adjoint_out: float32 [4, 1, 2, 128, 128, 128], P('ka', None, None, 'fft')
- cross_potential: float32 [128, 128, 128], P('fft')
The draws below stay inside these ranges and needn't reach their ends.
Inputs may be any that keep to these rules, and one draw needn't show every extreme that they name: `kpoint_weight`: symmetry multiplicities of the k-points.
All inputs are finite; a program needn't handle non-finite values.
Results may differ from the reference program's by a relative error of at most 0.0003.
Values sent between devices are 32-bit elements; how exact they have to be, the bound alone decides.
A program may use at most 128 MiB of HBM per device.

```python
import math
import jax
import jax.numpy as jnp

N = 128
BANDS = 1
STEPS = 2
SUB = 4
KPTS = 4


def place_ends(array, key, least, high):
    shape = array.shape
    spot = [jax.random.randint(jax.random.fold_in(key, axis), (), 0, shape[axis]) for axis in range(len(shape))]
    array = array.at[tuple(spot)].set(least)
    longest = shape.index(max(shape))
    spot[longest] = (spot[longest] + 1) % shape[longest]
    return array.at[tuple(spot)].set(high)


def block_scale(rng, dims, pieces, smallest, high):
    gain, own = 1.0, jax.random.fold_in(rng, 6)
    for position, parts in pieces:
        draws = jnp.exp(jax.random.uniform(jax.random.fold_in(own, position), (parts,), jnp.float32, smallest / len(pieces), high / len(pieces)))
        gain = gain * jnp.repeat(draws, dims[position] // parts).reshape([-1 if axis == position else 1 for axis in range(len(dims))])
    return gain


def bell_draw(own_key, shape, scale, bound, shards=(), held_as=jnp.bfloat16):
    array = scale * jax.random.normal(own_key, shape, jnp.float32)
    if shards:
        array = array * block_scale(own_key, shape, shards, -0.22, 0.18)
    return jnp.clip(array, -bound, bound).astype(held_as)


def setup_inputs(seed: int = 0) -> dict:
    splits = jax.random.split(jax.random.key(seed), 8)
    orbitals = bell_draw(splits[0], (KPTS, BANDS, 2, N, N, N), 0.5, 3.0, ((0, 4), (3, 64)), jnp.float32)
    costate = bell_draw(splits[1], (KPTS, BANDS, 2, N, N, N), 1.0, 6.0, ((0, 4), (3, 64)), jnp.float32)
    potential = bell_draw(splits[2], (N, N, N), 1.0, 4.0, ((0, 64),), jnp.float32)
    xc_kernel = jnp.clip(-1.0 + 0.9 * jax.random.uniform(splits[3], (N, N, N), jnp.float32) ** block_scale(splits[3], (N, N, N), ((0, 64),), -0.2, 0.2), -1.0, -0.1)
    vector_potential = jnp.clip(jax.random.uniform(splits[4], (STEPS * SUB,), jnp.float32, -0.6, 0.6), -0.6, 0.6)
    kpoint_weight = place_ends(jax.random.randint(splits[5], (KPTS,), 1, 9), jax.random.fold_in(splits[5], 1), 1, 8).astype(jnp.int32)
    occupation = jax.random.randint(splits[6], (BANDS,), 100, 201).astype(jnp.int32)
    return {"orbitals": orbitals, "costate": costate, "potential": potential, "xc_kernel": xc_kernel, "vector_potential": vector_potential, "kpoint_weight": kpoint_weight, "occupation": occupation}


spacing = 0.25
step_time = 0.6


def wave_numbers(grid_size):
    grid_line = jnp.arange(grid_size)
    signed_line = jnp.where(grid_line < grid_size // 2, grid_line, grid_line - grid_size)
    return (2.0 * math.pi / (grid_size * spacing)) * signed_line.astype(jnp.float32)


def substep(field, potential, shift_x, shift_y, shift_z, numbers, push_value, time_sign):
    sub_time = step_time / SUB
    potential_phase = jnp.exp(-1j * time_sign * (0.5 * sub_time) * potential)
    field = field * potential_phase
    spectrum = jnp.fft.fftn(field, axes=(-3, -2, -1))
    along_x = shift_x[:, None, None, None] + numbers[None, :, None, None] + push_value
    along_y = shift_y + numbers[None, None, :, None]
    along_z = shift_z + numbers[None, None, None, :]
    kinetic_angle = (0.5 * sub_time) * (along_x * along_x + along_y * along_y + along_z * along_z)
    spectrum = spectrum * jnp.exp(-1j * time_sign * kinetic_angle)[:, None]
    field = jnp.fft.ifftn(spectrum, axes=(-3, -2, -1))
    return field * potential_phase


def reference(orbitals, costate, potential, xc_kernel, vector_potential, kpoint_weight, occupation):
    lattice_unit = 2.0 * math.pi / (N * spacing)
    k_points = jnp.arange(KPTS).astype(jnp.float32)
    shift_x = lattice_unit * ((k_points + 0.5) / KPTS - 0.5)
    shift_y = lattice_unit * 0.25
    shift_z = -lattice_unit * 0.25
    numbers = wave_numbers(N)
    orbital_field = orbitals[:, :, 0] + 1j * orbitals[:, :, 1]
    history = [orbital_field]
    for step_index in range(STEPS):
        for sub_index in range(SUB):
            orbital_field = substep(orbital_field, potential, shift_x, shift_y, shift_z, numbers,
                                    vector_potential[step_index * SUB + sub_index], 1.0)
        history.append(orbital_field)
    weight = kpoint_weight.astype(jnp.float32) / jnp.sum(kpoint_weight).astype(jnp.float32)
    occupied = occupation.astype(jnp.float32) / 100.0
    band_factor = 2.0 * weight[:, None] * occupied[None, :]
    g_squared = (numbers[:, None, None] * numbers[:, None, None] + numbers[None, :, None] * numbers[None, :, None]
                 + numbers[None, None, :] * numbers[None, None, :])
    coulomb = jnp.where(g_squared > 0, 4.0 * math.pi / jnp.where(g_squared > 0, g_squared, 1.0), 0.0)
    adjoint_field = costate[:, :, 0] + 1j * costate[:, :, 1]
    cross_pot = jnp.zeros_like(potential)
    for step_index in range(STEPS - 1, -1, -1):
        forward_field = history[step_index + 1]
        intersection = jnp.real(adjoint_field) * jnp.real(forward_field) + jnp.imag(adjoint_field) * jnp.imag(forward_field)
        density = jnp.sum(band_factor[:, :, None, None, None] * intersection, axis=(0, 1))
        hartree_pot = jnp.real(jnp.fft.ifftn(coulomb * jnp.fft.fftn(density)))
        cross_pot = hartree_pot + xc_kernel * density
        adjoint_field = adjoint_field - 1j * step_time * cross_pot * forward_field
        for sub_index in range(SUB - 1, -1, -1):
            adjoint_field = substep(adjoint_field, potential, shift_x, shift_y, shift_z, numbers,
                                    vector_potential[step_index * SUB + sub_index], -1.0)
    result_field = jnp.stack([jnp.real(adjoint_field), jnp.imag(adjoint_field)], axis=2)
    return result_field, cross_pot
```

```python
import functools
import math

import jax
import jax.numpy as jnp
import ml_dtypes
import numpy as np
from jax import lax
from jax.experimental import pallas as pl
from jax.experimental.pallas import tpu as pltpu
from jax.sharding import PartitionSpec as P

MESH = pl.DeviceIdType.MESH
N = 128
H = 64
STEPS = 2
SUB = 4
KPTS = 4
spacing = 0.25
step_time = 0.6
SUB_TIME = step_time / SUB
UNIT = 2.0 * math.pi / (N * spacing)
BF = jnp.bfloat16
F32 = jnp.float32
PARTS = [(o, f, c) for o in range(2) for f in range(2) for c in range(2)]


def split(matrix):
    high = matrix.astype(np.float32).astype(ml_dtypes.bfloat16)
    low = (matrix - high.astype(np.float64)).astype(np.float32).astype(ml_dtypes.bfloat16)
    return high, low


def constants():
    line = np.arange(N)
    signed = np.where(line < H, line, line - N)
    forward = np.exp(-2j * np.pi / N * ((line[:, None] * line[None, :]) % N))
    inverse = forward.conj().T / N
    order = np.array([c * N + 2 * q + f for f in range(2) for c in range(2) for q in range(H)])

    def stacked(matrix):
        return np.block([[matrix.real, -matrix.imag], [matrix.imag, matrix.real]])

    square = []
    for shift, side in ((0.25, "left"), (-0.25, "right")):
        wave = UNIT * (shift + signed)
        for sign in (1.0, -1.0):
            phase = np.exp(-1j * sign * 0.5 * SUB_TIME * wave * wave)
            full = stacked(inverse @ (phase[:, None] * forward))
            full = full[order][:, order] if side == "left" else full.T
            square += list(split(full))
    square += list(split(stacked(inverse)[order]))
    dft = stacked(forward)[:, order].astype(np.float32)

    real = np.zeros((N, N))
    real[0] = 1.0 / math.sqrt(N)
    real[N - 1] = np.cos(np.pi * line) / math.sqrt(N)
    for k in range(1, H):
        real[2 * k - 1] = math.sqrt(2.0 / N) * np.cos(2.0 * np.pi * (k * line % N) / N)
        real[2 * k] = math.sqrt(2.0 / N) * np.sin(2.0 * np.pi * (k * line % N) / N)
    pairs = np.array([2 * q + f for f in range(2) for q in range(H)])
    small = []
    for matrix in (real[:, pairs], real[:, pairs].T, real.T, real):
        small += list(split(matrix))
    return np.stack(square), dft, np.stack(small)


AY, BZ, FINV = 0, 4, 8
R_IN, R_OUT, R_RIGHT, R_BACK = 0, 2, 4, 6


def halves(value):
    high = value.astype(BF)
    return high, (value - high.astype(F32)).astype(BF)


def dot(a, b):
    return jnp.dot(a, b, preferred_element_type=F32)


def mul_left(high, low, value):
    vh, vl = halves(value)
    return dot(high, vh) + (dot(high, vl) + dot(low, vh))


def mul_right(value, high, low):
    vh, vl = halves(value)
    return dot(vh, high) + (dot(vl, high) + dot(vh, low))


def cat(values, axis):
    return jnp.concatenate(values, axis=axis)


def left(high, low, field):
    rows = [cat([field[0, f, c], field[1, f, c]], 1) for f in range(2) for c in range(2)]
    out = mul_left(high, low, cat(rows, 0))
    return {
        (o, f, c): out[(f * 2 + c) * H : (f * 2 + c + 1) * H, o * N : (o + 1) * N]
        for o, f, c in PARTS
    }


def right(high, low, field):
    rows = [cat([field[o, f, 0], field[o, f, 1]], 1) for o in range(2) for f in range(2)]
    out = mul_right(cat(rows, 0), high, low)
    return {
        (o, f, c): out[(o * 2 + f) * H : (o * 2 + f + 1) * H, c * N : (c + 1) * N]
        for o, f, c in PARTS
    }


def rotate(field, phase, sign):
    out = {}
    for o in range(2):
        for f in range(2):
            cosine, sine = phase[o, f, 0], sign * phase[o, f, 1]
            re, im = field[o, f, 0], field[o, f, 1]
            out[o, f, 0] = re * cosine + im * sine
            out[o, f, 1] = im * cosine - re * sine
    return out


def double(phase):
    out = {}
    for o in range(2):
        for f in range(2):
            cosine, sine = phase[o, f, 0], phase[o, f, 1]
            out[o, f, 0] = cosine * cosine - sine * sine
            out[o, f, 1] = 2.0 * cosine * sine
    return out


def read(ref):
    return {(o, f, c): ref[pl.ds((o * 4 + f * 2 + c) * H, H), :] for o, f, c in PARTS}


def write(ref, field):
    for o, f, c in PARTS:
        ref[pl.ds((o * 4 + f * 2 + c) * H, H), :] = field[o, f, c]


def read_tiles(ref):
    return {(o, f, c): ref[pl.ds(o * 4 + f * 2 + c, H, stride=8), :] for o, f, c in PARTS}


def write_tiles(ref, field):
    for o, f, c in PARTS:
        ref[pl.ds(f * 4 + o * 2 + c, H, stride=8), :] = field[o, f, c]


def read_planes(ref):
    return {(o, f, c): ref[pl.ds((c * 2 + o) * N + f, H, stride=2), :] for o, f, c in PARTS}


def plane_phase(ref):
    out = {}
    for o in range(2):
        for f in range(2):
            angle = (0.5 * SUB_TIME) * ref[pl.ds(o * N + f, H, stride=2), :]
            out[o, f, 0] = jnp.cos(angle)
            out[o, f, 1] = jnp.sin(angle)
    return out


def kernel(
    orb, cost, pot, xck, vec, weight, occupation, square, dft, small,
    out, cross_out,
    send, recv0, recv1, recv_last, phase_send, phase_recv, cost_recv, pot_recv, xck_recv,
    orig_phase, plane_one, plane_two, col_two, cur, psi_one, psi, adj, first, second,
    coulomb, h_send, h_recv, b_send, b_recv, cross_stage, cross_recv,
    send_sem, recv_sem, last_sem, phase_sem, move_send, move_recv,
    h_send_sem, h_recv_sem, b_send_sem, b_recv_sem, known,
):
    ka = lax.axis_index("ka")
    fft = lax.axis_index("fft")
    block = fft // 16
    member = (fft % 16) * 4 + ka
    ident = fft * 4 + ka
    home = block == ka

    def place(p):
        return (p % 4, p // 4)

    def remote(src, dst, ss, rs, device):
        return pltpu.make_async_remote_copy(
            src_ref=src, dst_ref=dst, send_sem=ss, recv_sem=rs, device_id=device, device_id_type=MESH
        )

    def wait_rows(ref, rows, sem):
        part = ref.at[pl.ds(0, rows)]
        pltpu.make_async_copy(part, part, sem).wait()

    def tile(ref, index, rows=8):
        return ref.at[pl.ds(pl.multiple_of(index * rows, rows), rows)]

    barrier = pltpu.get_barrier_semaphore()

    def greet(d, carry):
        peer = jnp.bitwise_xor(fft, d)

        @pl.when(jnp.logical_or(block != ka, d != 0))
        def _():
            pl.semaphore_signal(barrier, inc=1, device_id=(block, peer), device_id_type=MESH)

        return carry

    lax.fori_loop(0, 64, greet, 0)

    phase = plane_phase(pot)
    write(orig_phase, phase)
    write_tiles(phase_send, phase)
    field = rotate(read_planes(orb), phase, 1.0)
    field = right(square[BZ], square[BZ + 1], field)
    field = left(square[AY], square[AY + 1], field)
    write_tiles(send, field)

    @pl.when(home)
    def _():
        pl.semaphore_wait(barrier, 63)

    @pl.when(jnp.logical_not(home))
    def _():
        pl.semaphore_wait(barrier, 64)

    def start_first(d, carry):
        p = jnp.bitwise_xor(member, d)
        own = jnp.logical_and(home, d == 0)

        @pl.when(jnp.logical_not(own))
        def _():
            device = place(ka * 64 + p)
            remote(tile(send, p), tile(recv0, fft), send_sem, recv_sem.at[0], device).start()

        @pl.when(own)
        def _():
            pltpu.make_async_copy(tile(send, p), tile(recv0, fft), recv_sem.at[0]).start()

        return carry

    lax.fori_loop(0, 64, start_first, 0)

    def start_phase(d, carry):
        p = jnp.bitwise_xor(member, d)
        own = jnp.logical_and(home, d == 0)

        @pl.when(jnp.logical_not(own))
        def _():
            device = place(ka * 64 + p)
            remote(
                tile(phase_send, p), tile(phase_recv, fft), phase_sem.at[0], phase_sem.at[1], device
            ).start()

        @pl.when(own)
        def _():
            pltpu.make_async_copy(
                tile(phase_send, p), tile(phase_recv, fft), phase_sem.at[1]
            ).start()

        return carry

    lax.fori_loop(0, 64, start_phase, 0)

    stay = jnp.logical_and(home, member == fft)
    moves = ((pot, pot_recv), (xck, xck_recv), (cost, cost_recv))
    for index, (src, dst) in enumerate(moves):

        @pl.when(stay)
        def _():
            pltpu.make_async_copy(src, dst, move_recv.at[index]).start()

        @pl.when(jnp.logical_not(stay))
        def _():
            remote(
                src, dst, move_send.at[index], move_recv.at[index], place(ka * 64 + fft)
            ).start()

    def wait_move(index):
        src, dst = moves[index]
        pltpu.make_async_copy(dst, dst, move_recv.at[index]).wait()

        @pl.when(jnp.logical_not(stay))
        def _():
            pltpu.make_async_copy(src, src, move_send.at[index]).wait()

    column = fft * 2 + ka // 2
    owner = ka % 2 == 0
    unit_y = (UNIT * ((column + 1) // 2)).astype(F32)
    along_x = (lax.broadcasted_iota(jnp.int32, (N, N), 0) + 1) // 2
    along_z = (lax.broadcasted_iota(jnp.int32, (N, N), 1) + 1) // 2
    wave_x = UNIT * along_x.astype(F32)
    wave_z = UNIT * along_z.astype(F32)
    g_squared = wave_x * wave_x + unit_y * unit_y + wave_z * wave_z
    positive = g_squared > 0
    coulomb[...] = jnp.where(positive, 4.0 * math.pi / jnp.where(positive, g_squared, 1.0), 0.0)

    shift_x = UNIT * ((block.astype(F32) + 0.5) / KPTS - 0.5)

    def build(target, sub_index, sign):
        mode = lax.broadcasted_iota(jnp.int32, (N, N), 0)
        mode = jnp.where(mode < H, mode, mode - N).astype(F32)
        wave = shift_x + UNIT * mode + vec[sub_index]
        angle = (0.5 * SUB_TIME) * (wave * wave)
        cosine, sine = jnp.cos(angle), sign * jnp.sin(angle)
        cosine, sine = cat([cosine, cosine], 1), cat([sine, sine], 1)
        re, im = dft[0:N, :], dft[N : 2 * N, :]
        turned = cat([re * cosine + im * sine, im * cosine - re * sine], 0)
        made = mul_left(square[FINV], square[FINV + 1], turned)
        high, low = halves(made)
        target[0] = high
        target[1] = low

    def start_inside(target, sem):
        def start(d, carry):
            p = jnp.bitwise_xor(member, d)
            remote(
                tile(send, p), tile(target, member), send_sem, sem, place(block * 64 + p)
            ).start()
            return carry

        lax.fori_loop(1, 64, start, 0)
        pltpu.make_async_copy(tile(send, member), tile(target, member), sem).start()

    def columns(i, sign):
        forward = i < 4
        build(first, jnp.where(forward, 2 * i, 15 - 2 * i), sign)
        build(second, jnp.where(forward, 2 * i + 1, 14 - 2 * i), sign)
        wait_rows(recv0, 512, recv_sem.at[0])

        @pl.when(jnp.logical_and(i == 0, jnp.logical_not(home)))
        def _():
            wait_rows(send, 512, send_sem)

        @pl.when(jnp.logical_or(i > 0, home))
        def _():
            wait_rows(send, 504, send_sem)

        @pl.when(i == 0)
        def _():
            wait_rows(phase_recv, 512, phase_sem.at[1])
            write(col_two, double(read_tiles(phase_recv)))

            @pl.when(ka == 0)
            def _():
                for step in range(1, 4):
                    other = (block + step) % 4
                    pl.semaphore_signal(
                        known, inc=1, device_id=(block, other * 16 + fft % 16), device_id_type=MESH
                    )

        field = left(first[0], first[1], read_tiles(recv0))
        field = rotate(field, read(col_two), sign)
        field = left(second[0], second[1], field)
        back = jnp.where(forward, BZ, BZ + 2)
        field = right(square[back], square[back + 1], field)
        write_tiles(send, field)

    def response(last):
        wave, other = read(psi), read(adj)
        total = weight[0] + weight[1] + weight[2] + weight[3]
        share = weight[block].astype(F32) / total.astype(F32)
        factor = 2.0 * share * (occupation[0].astype(F32) / 100.0)
        own = {
            (o, f): factor * (other[o, f, 0] * wave[o, f, 0] + other[o, f, 1] * wave[o, f, 1])
            for o in range(2)
            for f in range(2)
        }
        dense = cat([cat([own[0, f], own[1, f]], 1) for f in range(2)], 0)
        dense = mul_left(small[R_IN], small[R_IN + 1], dense)
        dense = mul_right(
            cat([dense[:, 0:N], dense[:, N : 2 * N]], 0), small[R_RIGHT], small[R_RIGHT + 1]
        )
        for o in range(2):
            h_send[pl.ds(o, N, stride=2), :] = dense[o * N : (o + 1) * N]

        def start_dense(d, carry):
            to = (column + d) % N
            device = ((to % 2) * 2, to // 2)
            mine = jnp.logical_and(owner, d == 0)

            @pl.when(jnp.logical_not(mine))
            def _():
                remote(
                    tile(h_send, to, 2), tile(h_recv, ident, 2), h_send_sem, h_recv_sem, device
                ).start()

            @pl.when(mine)
            def _():
                pltpu.make_async_copy(
                    tile(h_send, to, 2), tile(h_recv, ident, 2), h_recv_sem
                ).start()

            return carry

        lax.fori_loop(0, N, start_dense, 0)

        @pl.when(owner)
        def _():
            wait_rows(h_recv, 512, h_recv_sem)
            summed = []
            for f in range(2):
                terms = [h_recv[pl.ds(k * N + f, H, stride=2), :] for k in range(4)]
                summed.append((terms[0] + terms[1]) + (terms[2] + terms[3]))
            line = mul_left(small[R_IN], small[R_IN + 1], cat(summed, 0)) * coulomb[...]
            line = mul_left(small[R_OUT], small[R_OUT + 1], line)
            for f in range(2):
                b_send[pl.ds(f, H, stride=4), :] = line[f * H : (f + 1) * H]
                b_send[pl.ds(2 + f, H, stride=4), :] = summed[f]
            for group in range(4):
                there = (block + group) % 4

                def start_back(d, carry, group=group, there=there):
                    p = jnp.bitwise_xor(member, d)
                    mine = jnp.logical_and(group == 0, d == 0)

                    @pl.when(jnp.logical_not(mine))
                    def _():
                        remote(
                            tile(b_send, p, 4),
                            tile(b_recv, column, 4),
                            b_send_sem.at[group],
                            b_recv_sem,
                            place(there * 64 + p),
                        ).start()

                    @pl.when(mine)
                    def _():
                        pltpu.make_async_copy(
                            tile(b_send, p, 4), tile(b_recv, column, 4), b_recv_sem
                        ).start()

                    return carry

                lax.fori_loop(0, 64, start_back, 0)

        wait_rows(b_recv, 512, b_recv_sem)
        parts = [b_recv[pl.ds(r, N, stride=4), :] for r in range(4)]
        parts = mul_right(cat(parts, 0), small[R_BACK], small[R_BACK + 1])
        parts = cat([parts[r * N : (r + 1) * N] for r in range(4)], 1)
        parts = mul_left(small[R_OUT], small[R_OUT + 1], parts)
        for o in range(2):
            for f in range(2):
                rows = slice(f * H, (f + 1) * H)
                hartree = parts[rows, o * N : (o + 1) * N]
                density = parts[rows, (2 + o) * N : (3 + o) * N]
                cross = hartree + xck_recv[pl.ds(o * N + f, H, stride=2), :] * density
                cross_stage[pl.ds(o * N + f, H, stride=2), :] = cross
                base = (o * 4 + f * 2) * H
                cur[pl.ds(base, H), :] = other[o, f, 0] + step_time * cross * wave[o, f, 1]
                cur[pl.ds(base + H, H), :] = other[o, f, 1] - step_time * cross * wave[o, f, 0]

        @pl.when(owner)
        def _():
            wait_rows(h_send, 254, h_send_sem)
            wait_rows(b_send, 252, b_send_sem.at[0])
            for group in range(1, 4):
                wait_rows(b_send, 256, b_send_sem.at[group])

        @pl.when(jnp.logical_not(owner))
        def _():
            wait_rows(h_send, 256, h_send_sem)

        @pl.when(last)
        def _():
            @pl.when(stay)
            def _():
                pltpu.make_async_copy(cross_stage, cross_recv, move_recv.at[3]).start()

            @pl.when(jnp.logical_not(stay))
            def _():
                remote(
                    cross_stage, cross_recv, move_send.at[3], move_recv.at[3], (block, member)
                ).start()

    def pair(i, carry):
        sign = jnp.where(i < 4, 1.0, -1.0).astype(F32)
        columns(i, sign)
        start_inside(recv1, recv_sem.at[1])

        @pl.when(i == 0)
        def _():
            wait_move(0)
            phase = plane_phase(pot_recv)
            write(plane_one, phase)
            write(plane_two, double(phase))
            wait_move(1)

        wait_rows(recv1, 512, recv_sem.at[1])
        wait_rows(send, 504, send_sem)
        turn = jnp.where(i < 4, AY, AY + 2)
        field = left(square[turn], square[turn + 1], read_tiles(recv1))

        @pl.when(i % 2 == 0)
        def _():
            write(cur, rotate(field, read(plane_two), sign))

        @pl.when(i % 2 == 1)
        def _():
            write(cur, rotate(field, read(plane_one), sign))

        @pl.when(i == 1)
        def _():
            psi_one[...] = cur[...]

        @pl.when(i == 3)
        def _():
            wait_move(2)
            psi[...] = cur[...]
            write(adj, read_planes(cost_recv))

        @pl.when(i == 5)
        def _():
            psi[...] = psi_one[...]
            adj[...] = cur[...]

        @pl.when(jnp.logical_or(i == 3, i == 5))
        def _():
            response(i == 5)

        sign_next = jnp.where(i < 3, 1.0, -1.0).astype(F32)

        @pl.when(i % 2 == 1)
        def _():
            write(cur, rotate(read(cur), read(plane_one), sign_next))

        turn = jnp.where(i < 3, AY, AY + 2)
        back = jnp.where(i < 3, BZ, BZ + 2)
        field = right(square[back], square[back + 1], read(cur))
        field = left(square[turn], square[turn + 1], field)
        write_tiles(send, field)

        @pl.when(jnp.logical_and(i == 0, jnp.logical_not(home)))
        def _():
            pl.semaphore_wait(known, 1)

        start_inside(recv0, recv_sem.at[0])
        return carry

    lax.fori_loop(0, 7, pair, 0)

    columns(jnp.int32(7), jnp.float32(-1.0))

    def start_last(d, carry):
        q = jnp.bitwise_xor(fft, d)
        own = jnp.logical_and(home, d == 0)

        @pl.when(jnp.logical_not(own))
        def _():
            remote(
                tile(send, q), tile(recv_last, member), send_sem, last_sem, (block, q)
            ).start()

        @pl.when(own)
        def _():
            pltpu.make_async_copy(tile(send, q), tile(recv_last, member), last_sem).start()

        return carry

    lax.fori_loop(0, 64, start_last, 0)

    pltpu.make_async_copy(cross_recv, cross_recv, move_recv.at[3]).wait()
    cross_out[...] = cross_recv[...]

    @pl.when(jnp.logical_not(stay))
    def _():
        pltpu.make_async_copy(cross_stage, cross_stage, move_send.at[3]).wait()

    wait_rows(recv_last, 512, last_sem)
    field = left(square[AY + 2], square[AY + 3], read_tiles(recv_last))
    field = rotate(field, read(orig_phase), -1.0)
    for o, f, c in PARTS:
        out[pl.ds((c * 2 + o) * N + f, H, stride=2), :] = field[o, f, c]

    @pl.when(home)
    def _():
        wait_rows(send, 504, send_sem)
        wait_rows(phase_send, 504, phase_sem.at[0])

    @pl.when(jnp.logical_not(home))
    def _():
        wait_rows(send, 512, send_sem)
        wait_rows(phase_send, 512, phase_sem.at[0])


def local(orbitals, costate, potential, xc_kernel, vector_potential, kpoint_weight, occupation):
    square, dft, small = constants()
    vmem = pl.BlockSpec(memory_space=pltpu.VMEM)
    smem = pl.BlockSpec(memory_space=pltpu.SMEM)

    def rows(count):
        return pltpu.VMEM((count, N), F32)

    field = rows(512)
    half = rows(256)
    dma = pltpu.SemaphoreType.DMA
    out, cross = pl.pallas_call(
        kernel,
        out_shape=(
            jax.ShapeDtypeStruct((512, N), F32),
            jax.ShapeDtypeStruct((256, N), F32),
        ),
        in_specs=[vmem] * 4 + [smem] * 3 + [vmem] * 3,
        out_specs=(vmem, vmem),
        scratch_shapes=[
            field, field, field, field, field, field, field, half, half,
            field, field, field, field, field, field, field, field,
            pltpu.VMEM((2, 256, 256), BF), pltpu.VMEM((2, 256, 256), BF),
            rows(N), half, field, half, field, half, half,
            dma, dma((2,)), dma, dma((2,)), dma((4,)), dma((4,)),
            dma, dma, dma((4,)), dma, pltpu.SemaphoreType.REGULAR,
        ],
        compiler_params=pltpu.CompilerParams(
            collective_id=0, has_side_effects=True, vmem_limit_bytes=40 * 1024 * 1024
        ),
        name="window",
    )(
        orbitals.reshape(512, N),
        costate.reshape(512, N),
        potential.reshape(256, N),
        xc_kernel.reshape(256, N),
        vector_potential,
        kpoint_weight,
        occupation,
        jnp.asarray(square),
        jnp.asarray(dft),
        jnp.asarray(small),
    )
    return out.reshape(orbitals.shape), cross.reshape(potential.shape)


def solution(mesh):
    placed = (
        P("ka", None, None, "fft", None, None),
        P("ka", None, None, "fft", None, None),
        P("fft", None, None),
        P("fft", None, None),
        P(),
        P(),
        P(),
    )
    return jax.shard_map(
        local,
        mesh=mesh,
        in_specs=placed,
        out_specs=(P("ka", None, None, "fft", None, None), P("fft", None, None)),
        check_vma=False,
    )
```

```python
import functools
import math

import jax
import jax.numpy as jnp
import ml_dtypes
import numpy as np
from jax import lax
from jax.experimental import pallas as pl
from jax.experimental.pallas import tpu as pltpu
from jax.sharding import PartitionSpec as P

MESH = pl.DeviceIdType.MESH
N = 128
H = 64
STEPS = 2
SUB = 4
FAR = 52
KPTS = 4
spacing = 0.25
step_time = 0.6
SUB_TIME = step_time / SUB
UNIT = 2.0 * math.pi / (N * spacing)
BF = jnp.bfloat16
F32 = jnp.float32
PARTS = [(o, f, c) for o in range(2) for f in range(2) for c in range(2)]


def swap(index):
    return (index % 2) * 2 + index // 2


def slot_of(pair):
    return (pair // 32) * 32 + ((pair // 2) % 4) * 8 + (pair % 2) * 4 + (pair // 8) % 4


def plane_of(slot):
    return (slot // 32) * 32 + (slot % 4) * 8 + ((slot // 8) % 4) * 2 + (slot // 4) % 2


def split(matrix):
    high = matrix.astype(np.float32).astype(ml_dtypes.bfloat16)
    low = (matrix - high.astype(np.float64)).astype(np.float32).astype(ml_dtypes.bfloat16)
    return high, low


def constants():
    line = np.arange(N)
    signed = np.where(line < H, line, line - N)
    forward = np.exp(-2j * np.pi / N * ((line[:, None] * line[None, :]) % N))
    inverse = forward.conj().T / N
    order = np.array([c * N + 2 * q + f for f in range(2) for c in range(2) for q in range(H)])
    slots = [plane_of(q) for q in range(H)]
    order_x = np.array([c * N + 2 * q + f for f in range(2) for c in range(2) for q in slots])

    def stacked(matrix):
        return np.block([[matrix.real, -matrix.imag], [matrix.imag, matrix.real]])

    square = []
    for shift, side in ((0.25, "left"), (-0.25, "right")):
        wave = UNIT * (shift + signed)
        for sign in (1.0, -1.0):
            phase = np.exp(-1j * sign * 0.5 * SUB_TIME * wave * wave)
            full = stacked(inverse @ (phase[:, None] * forward))
            full = full[order][:, order] if side == "left" else full.T
            square += list(split(full))
    square += list(split(stacked(inverse)[order_x]))
    dft = stacked(forward)[:, order_x].astype(np.float32)

    real = np.zeros((N, N))
    real[0] = 1.0 / math.sqrt(N)
    real[N - 1] = np.cos(np.pi * line) / math.sqrt(N)
    for k in range(1, H):
        real[2 * k - 1] = math.sqrt(2.0 / N) * np.cos(2.0 * np.pi * (k * line % N) / N)
        real[2 * k] = math.sqrt(2.0 / N) * np.sin(2.0 * np.pi * (k * line % N) / N)
    pairs = np.array([2 * q + f for f in range(2) for q in range(H)])
    pairs_x = np.array([2 * q + f for f in range(2) for q in slots])
    small = []
    for matrix in (
        real[:, pairs], real[:, pairs].T, real.T, real, real[:, pairs_x], real[:, pairs_x].T,
    ):
        small += list(split(matrix))
    return np.stack(square), dft, np.stack(small)


AY, BZ, FINV = 0, 4, 8
R_IN, R_OUT, R_RIGHT, R_BACK, X_IN, X_OUT = 0, 2, 4, 6, 8, 10


def halves(value):
    high = value.astype(BF)
    return high, (value - high.astype(F32)).astype(BF)


def dot(a, b):
    return jnp.dot(a, b, preferred_element_type=F32)


def mul_left(high, low, value):
    vh, vl = halves(value)
    return dot(high, vh) + (dot(high, vl) + dot(low, vh))


def mul_right(value, high, low):
    vh, vl = halves(value)
    return dot(vh, high) + (dot(vl, high) + dot(vh, low))


def cat(values, axis):
    return jnp.concatenate(values, axis=axis)


def left(high, low, field):
    rows = [cat([field[0, f, c], field[1, f, c]], 1) for f in range(2) for c in range(2)]
    out = mul_left(high, low, cat(rows, 0))
    return {
        (o, f, c): out[(f * 2 + c) * H : (f * 2 + c + 1) * H, o * N : (o + 1) * N]
        for o, f, c in PARTS
    }


def right(high, low, field):
    rows = [cat([field[o, f, 0], field[o, f, 1]], 1) for o in range(2) for f in range(2)]
    out = mul_right(cat(rows, 0), high, low)
    return {
        (o, f, c): out[(o * 2 + f) * H : (o * 2 + f + 1) * H, c * N : (c + 1) * N]
        for o, f, c in PARTS
    }


def rotate(field, phase, sign):
    out = {}
    for o in range(2):
        for f in range(2):
            cosine, sine = phase[o, f, 0], sign * phase[o, f, 1]
            re, im = field[o, f, 0], field[o, f, 1]
            out[o, f, 0] = re * cosine + im * sine
            out[o, f, 1] = im * cosine - re * sine
    return out


def double(phase):
    out = {}
    for o in range(2):
        for f in range(2):
            cosine, sine = phase[o, f, 0], phase[o, f, 1]
            out[o, f, 0] = cosine * cosine - sine * sine
            out[o, f, 1] = 2.0 * cosine * sine
    return out


def read(ref):
    return {(o, f, c): ref[pl.ds((o * 4 + f * 2 + c) * H, H), :] for o, f, c in PARTS}


def write(ref, field):
    for o, f, c in PARTS:
        ref[pl.ds((o * 4 + f * 2 + c) * H, H), :] = field[o, f, c]


def read_tiles(ref):
    return {(o, f, c): ref[pl.ds(o * 4 + f * 2 + c, H, stride=8), :] for o, f, c in PARTS}


def write_tiles(ref, field):
    for o, f, c in PARTS:
        ref[pl.ds(f * 4 + o * 2 + c, H, stride=8), :] = field[o, f, c]


def read_planes(ref):
    return {(o, f, c): ref[pl.ds((c * 2 + o) * N + f, H, stride=2), :] for o, f, c in PARTS}


def phase_of(angles):
    out = {}
    for (o, f), angle in angles.items():
        out[o, f, 0] = jnp.cos(angle)
        out[o, f, 1] = jnp.sin(angle)
    return out


def plane_values(ref, factor):
    return {
        (o, f): factor * ref[pl.ds(o * N + f, H, stride=2), :] for o in range(2) for f in range(2)
    }


def column_values(ref, factor):
    return {
        (o, f): factor * ref[pl.ds(o * 2 + f, H, stride=4), :] for o in range(2) for f in range(2)
    }


def kernel(
    orb_in, cost, pot_in, xck, vec, weight, occupation, square_in, dft_in, small_in,
    out, cross_out,
    orb, pot, square, dft, small,
    send, recv0, recv1, recv_last, column_send, column_recv, cost_recv, pot_recv, xck_recv,
    orig_phase, plane_one, plane_two, col_two, cur, psi_one, psi, adj, first, second,
    coulomb, h_send, h_recv, b_send, b_recv, cross_stage, cross_recv,
    load_sem, send_sem, recv_sem, last_sem, phase_sem, move_send, move_recv,
    h_send_sem, h_recv_sem, b_send_sem, b_recv_sem, known,
):
    ka = lax.axis_index("ka")
    fft = lax.axis_index("fft")
    block = fft // 16
    member = (fft % 16) * 4 + ka
    ident = fft * 4 + ka
    point = swap(block)
    goal = swap(ka)
    home = block == goal
    slot = slot_of(fft)
    plane = plane_of(member)
    stay = jnp.logical_and(home, member == slot)

    def place(p):
        return (p % 4, p // 4)

    def remote(src, dst, ss, rs, device):
        return pltpu.make_async_remote_copy(
            src_ref=src, dst_ref=dst, send_sem=ss, recv_sem=rs, device_id=device, device_id_type=MESH
        )

    def wait_rows(ref, rows, sem):
        part = ref.at[pl.ds(0, rows)]
        pltpu.make_async_copy(part, part, sem).wait()

    def tile(ref, index, rows=8):
        return ref.at[pl.ds(pl.multiple_of(index * rows, rows), rows)]

    loads = [
        pltpu.make_async_copy(src, dst, load_sem.at[index])
        for index, (src, dst) in enumerate(
            ((pot_in, pot), (orb_in, orb), (square_in, square), (dft_in, dft), (small_in, small))
        )
    ]
    for load in loads:
        load.start()

    barrier = pltpu.get_barrier_semaphore()

    def greet(d, carry):
        peer = jnp.bitwise_xor(fft, d)

        @pl.when(jnp.logical_not(jnp.logical_and(home, d == 0)))
        def _():
            pl.semaphore_signal(barrier, inc=1, device_id=(point, peer), device_id_type=MESH)

        return carry

    lax.fori_loop(0, 64, greet, 0)

    loads[0].wait()
    for o in range(2):
        for f in range(2):
            column_send[pl.ds(f * 2 + o, H, stride=4), :] = pot[pl.ds(o * N + f, H, stride=2), :]
    phase = phase_of(plane_values(pot, 0.5 * SUB_TIME))
    write(orig_phase, phase)
    loads[1].wait()
    field = rotate(read_planes(orb), phase, 1.0)
    loads[2].wait()
    field = right(square[BZ], square[BZ + 1], field)
    field = left(square[AY], square[AY + 1], field)
    write_tiles(send, field)

    @pl.when(home)
    def _():
        pl.semaphore_wait(barrier, 63)

    @pl.when(jnp.logical_not(home))
    def _():
        pl.semaphore_wait(barrier, 64)

    def start_first(src, dst, rows, ss, rs):
        def start(d, carry):
            p = jnp.bitwise_xor(member, jnp.bitwise_xor(d, FAR))
            own = jnp.logical_and(home, d == FAR)

            @pl.when(jnp.logical_not(own))
            def _():
                device = place(goal * 64 + p)
                remote(tile(src, p, rows), tile(dst, slot, rows), ss, rs, device).start()

            @pl.when(own)
            def _():
                pltpu.make_async_copy(tile(src, p, rows), tile(dst, slot, rows), rs).start()

            return carry

        lax.fori_loop(0, 64, start, 0)

    start_first(send, recv0, 8, send_sem, recv_sem.at[0])
    start_first(column_send, column_recv, 4, phase_sem.at[0], phase_sem.at[1])

    def start_move(src, dst, index):
        @pl.when(stay)
        def _():
            pltpu.make_async_copy(src, dst, move_recv.at[index]).start()

        @pl.when(jnp.logical_not(stay))
        def _():
            device = place(goal * 64 + slot)
            remote(src, dst, move_send.at[index], move_recv.at[index], device).start()

    def wait_move(src, dst, index):
        pltpu.make_async_copy(dst, dst, move_recv.at[index]).wait()

        @pl.when(jnp.logical_not(stay))
        def _():
            pltpu.make_async_copy(src, src, move_send.at[index]).wait()

    column = fft * 2 + ka // 2
    owner = ka % 2 == 0
    unit_y = (UNIT * ((column + 1) // 2)).astype(F32)
    along_x = (lax.broadcasted_iota(jnp.int32, (N, N), 0) + 1) // 2
    along_z = (lax.broadcasted_iota(jnp.int32, (N, N), 1) + 1) // 2
    wave_x = UNIT * along_x.astype(F32)
    wave_z = UNIT * along_z.astype(F32)
    g_squared = wave_x * wave_x + unit_y * unit_y + wave_z * wave_z
    positive = g_squared > 0
    coulomb[...] = jnp.where(positive, 4.0 * math.pi / jnp.where(positive, g_squared, 1.0), 0.0)

    shift_x = UNIT * ((point.astype(F32) + 0.5) / KPTS - 0.5)

    def build(target, sub_index, sign):
        mode = lax.broadcasted_iota(jnp.int32, (N, N), 0)
        mode = jnp.where(mode < H, mode, mode - N).astype(F32)
        wave = shift_x + UNIT * mode + vec[sub_index]
        angle = (0.5 * SUB_TIME) * (wave * wave)
        cosine, sine = jnp.cos(angle), sign * jnp.sin(angle)
        cosine, sine = cat([cosine, cosine], 1), cat([sine, sine], 1)
        re, im = dft[0:N, :], dft[N : 2 * N, :]
        turned = cat([re * cosine + im * sine, im * cosine - re * sine], 0)
        made = mul_left(square[FINV], square[FINV + 1], turned)
        high, low = halves(made)
        target[0] = high
        target[1] = low

    def start_inside(target, sem):
        def start(d, carry):
            p = jnp.bitwise_xor(member, jnp.bitwise_xor(d, FAR))
            remote(
                tile(send, p), tile(target, member), send_sem, sem, place(block * 64 + p)
            ).start()
            return carry

        lax.fori_loop(0, FAR, start, 0)
        lax.fori_loop(FAR + 1, 64, start, 0)
        pltpu.make_async_copy(tile(send, member), tile(target, member), sem).start()

    def columns(i, sign):
        forward = i < 4

        @pl.when(i == 0)
        def _():
            loads[3].wait()
            loads[4].wait()

        build(first, jnp.where(forward, 2 * i, 15 - 2 * i), sign)
        build(second, jnp.where(forward, 2 * i + 1, 14 - 2 * i), sign)
        wait_rows(recv0, 512, recv_sem.at[0])

        @pl.when(jnp.logical_and(i == 0, jnp.logical_not(home)))
        def _():
            wait_rows(send, 512, send_sem)

        @pl.when(jnp.logical_or(i > 0, home))
        def _():
            wait_rows(send, 504, send_sem)

        @pl.when(i == 0)
        def _():
            start_move(pot_in, pot_recv, 0)
            wait_rows(column_recv, 256, phase_sem.at[1])
            write(col_two, phase_of(column_values(column_recv, SUB_TIME)))

            @pl.when(ka == 0)
            def _():
                for step in range(1, 4):
                    other = (block + step) % 4
                    pl.semaphore_signal(
                        known, inc=1, device_id=(point, other * 16 + fft % 16), device_id_type=MESH
                    )

        field = left(first[0], first[1], read_tiles(recv0))
        field = rotate(field, read(col_two), sign)
        field = left(second[0], second[1], field)
        back = jnp.where(forward, BZ, BZ + 2)
        field = right(square[back], square[back + 1], field)
        write_tiles(send, field)

    def response(last):
        wave, other = read(psi), read(adj)
        total = weight[0] + weight[1] + weight[2] + weight[3]
        share = weight[point].astype(F32) / total.astype(F32)
        factor = 2.0 * share * (occupation[0].astype(F32) / 100.0)
        own = {
            (o, f): factor * (other[o, f, 0] * wave[o, f, 0] + other[o, f, 1] * wave[o, f, 1])
            for o in range(2)
            for f in range(2)
        }
        dense = cat([cat([own[0, f], own[1, f]], 1) for f in range(2)], 0)
        dense = mul_left(small[R_IN], small[R_IN + 1], dense)
        dense = mul_right(
            cat([dense[:, 0:N], dense[:, N : 2 * N]], 0), small[R_RIGHT], small[R_RIGHT + 1]
        )
        for o in range(2):
            h_send[pl.ds(o, N, stride=2), :] = dense[o * N : (o + 1) * N]

        def start_dense(d, carry):
            to = (column + d) % N
            device = ((to % 2) * 2, to // 2)
            mine = jnp.logical_and(owner, d == 0)

            @pl.when(jnp.logical_not(mine))
            def _():
                remote(
                    tile(h_send, to, 2), tile(h_recv, ident, 2), h_send_sem, h_recv_sem, device
                ).start()

            @pl.when(mine)
            def _():
                pltpu.make_async_copy(
                    tile(h_send, to, 2), tile(h_recv, ident, 2), h_recv_sem
                ).start()

            return carry

        lax.fori_loop(0, N, start_dense, 0)

        @pl.when(owner)
        def _():
            wait_rows(h_recv, 512, h_recv_sem)
            summed = []
            for f in range(2):
                terms = [h_recv[pl.ds(k * N + f, H, stride=2), :] for k in range(4)]
                summed.append((terms[0] + terms[1]) + (terms[2] + terms[3]))
            line = mul_left(small[X_IN], small[X_IN + 1], cat(summed, 0)) * coulomb[...]
            line = mul_left(small[X_OUT], small[X_OUT + 1], line)
            for f in range(2):
                b_send[pl.ds(f, H, stride=4), :] = line[f * H : (f + 1) * H]
                b_send[pl.ds(2 + f, H, stride=4), :] = summed[f]
            for group in range(4):
                there = (block + group) % 4

                def start_back(d, carry, group=group, there=there):
                    p = jnp.bitwise_xor(member, d)
                    mine = jnp.logical_and(group == 0, d == 0)

                    @pl.when(jnp.logical_not(mine))
                    def _():
                        remote(
                            tile(b_send, p, 4),
                            tile(b_recv, column, 4),
                            b_send_sem.at[group],
                            b_recv_sem,
                            place(there * 64 + p),
                        ).start()

                    @pl.when(mine)
                    def _():
                        pltpu.make_async_copy(
                            tile(b_send, p, 4), tile(b_recv, column, 4), b_recv_sem
                        ).start()

                    return carry

                lax.fori_loop(0, 64, start_back, 0)

        @pl.when(jnp.logical_not(last))
        def _():
            wait_move(xck, xck_recv, 1)

        wait_rows(b_recv, 512, b_recv_sem)
        parts = [b_recv[pl.ds(r, N, stride=4), :] for r in range(4)]
        parts = mul_right(cat(parts, 0), small[R_BACK], small[R_BACK + 1])
        parts = cat([parts[r * N : (r + 1) * N] for r in range(4)], 1)
        parts = mul_left(small[R_OUT], small[R_OUT + 1], parts)
        for o in range(2):
            for f in range(2):
                rows = slice(f * H, (f + 1) * H)
                hartree = parts[rows, o * N : (o + 1) * N]
                density = parts[rows, (2 + o) * N : (3 + o) * N]
                cross = hartree + xck_recv[pl.ds(o * N + f, H, stride=2), :] * density
                cross_stage[pl.ds(o * N + f, H, stride=2), :] = cross
                base = (o * 4 + f * 2) * H
                cur[pl.ds(base, H), :] = other[o, f, 0] + step_time * cross * wave[o, f, 1]
                cur[pl.ds(base + H, H), :] = other[o, f, 1] - step_time * cross * wave[o, f, 0]

        @pl.when(owner)
        def _():
            wait_rows(h_send, 254, h_send_sem)
            wait_rows(b_send, 252, b_send_sem.at[0])
            for group in range(1, 4):
                wait_rows(b_send, 256, b_send_sem.at[group])

        @pl.when(jnp.logical_not(owner))
        def _():
            wait_rows(h_send, 256, h_send_sem)

        @pl.when(last)
        def _():
            @pl.when(stay)
            def _():
                pltpu.make_async_copy(cross_stage, cross_recv, move_recv.at[3]).start()

            @pl.when(jnp.logical_not(stay))
            def _():
                remote(
                    cross_stage, cross_recv, move_send.at[3], move_recv.at[3], (point, plane)
                ).start()

    def move_quarter(i, part):
        @pl.when(jnp.logical_or(i == 1, i == 2))
        def _():
            quarter = 2 * (i - 1) + part
            start_move(tile(cost, quarter, N), tile(cost_recv, quarter, N), 2)

    def pair(i, carry):
        sign = jnp.where(i < 4, 1.0, -1.0).astype(F32)
        columns(i, sign)
        start_inside(recv1, recv_sem.at[1])

        @pl.when(i == 0)
        def _():
            wait_move(pot_in, pot_recv, 0)
            phase = phase_of(plane_values(pot_recv, 0.5 * SUB_TIME))
            write(plane_one, phase)
            write(plane_two, double(phase))

        move_quarter(i, 0)

        wait_rows(recv1, 512, recv_sem.at[1])
        wait_rows(send, 504, send_sem)
        turn = jnp.where(i < 4, AY, AY + 2)
        field = left(square[turn], square[turn + 1], read_tiles(recv1))

        @pl.when(i % 2 == 0)
        def _():
            write(cur, rotate(field, read(plane_two), sign))

        @pl.when(i % 2 == 1)
        def _():
            write(cur, rotate(field, read(plane_one), sign))

        @pl.when(i == 1)
        def _():
            psi_one[...] = cur[...]

        @pl.when(i == 3)
        def _():
            start_move(xck, xck_recv, 1)
            wait_move(cost, cost_recv, 2)
            psi[...] = cur[...]
            write(adj, read_planes(cost_recv))

        @pl.when(i == 5)
        def _():
            psi[...] = psi_one[...]
            adj[...] = cur[...]

        @pl.when(jnp.logical_or(i == 3, i == 5))
        def _():
            response(i == 5)

        sign_next = jnp.where(i < 3, 1.0, -1.0).astype(F32)

        @pl.when(i % 2 == 1)
        def _():
            write(cur, rotate(read(cur), read(plane_one), sign_next))

        turn = jnp.where(i < 3, AY, AY + 2)
        back = jnp.where(i < 3, BZ, BZ + 2)
        field = right(square[back], square[back + 1], read(cur))
        field = left(square[turn], square[turn + 1], field)
        write_tiles(send, field)

        @pl.when(jnp.logical_and(i == 0, jnp.logical_not(home)))
        def _():
            pl.semaphore_wait(known, 1)

        start_inside(recv0, recv_sem.at[0])
        move_quarter(i, 1)
        return carry

    lax.fori_loop(0, 7, pair, 0)

    columns(jnp.int32(7), jnp.float32(-1.0))

    def start_last(d, carry):
        q = jnp.bitwise_xor(fft, d)
        own = jnp.logical_and(home, d == 0)

        @pl.when(jnp.logical_not(own))
        def _():
            remote(
                tile(send, slot_of(q)), tile(recv_last, member), send_sem, last_sem, (point, q)
            ).start()

        @pl.when(own)
        def _():
            pltpu.make_async_copy(
                tile(send, slot_of(q)), tile(recv_last, member), last_sem
            ).start()

        return carry

    lax.fori_loop(0, 64, start_last, 0)

    pltpu.make_async_copy(cross_recv, cross_recv, move_recv.at[3]).wait()
    cross_out[...] = cross_recv[...]

    @pl.when(jnp.logical_not(stay))
    def _():
        pltpu.make_async_copy(cross_stage, cross_stage, move_send.at[3]).wait()

    wait_rows(recv_last, 512, last_sem)
    field = left(square[AY + 2], square[AY + 3], read_tiles(recv_last))
    field = rotate(field, read(orig_phase), -1.0)
    for o, f, c in PARTS:
        out[pl.ds((c * 2 + o) * N + f, H, stride=2), :] = field[o, f, c]

    @pl.when(home)
    def _():
        wait_rows(send, 504, send_sem)
        wait_rows(column_send, 252, phase_sem.at[0])

    @pl.when(jnp.logical_not(home))
    def _():
        wait_rows(send, 512, send_sem)
        wait_rows(column_send, 256, phase_sem.at[0])


def local(orbitals, costate, potential, xc_kernel, vector_potential, kpoint_weight, occupation):
    square, dft, small = constants()
    vmem = pl.BlockSpec(memory_space=pltpu.VMEM)
    smem = pl.BlockSpec(memory_space=pltpu.SMEM)
    hbm = pl.BlockSpec(memory_space=pltpu.HBM)

    def rows(count):
        return pltpu.VMEM((count, N), F32)

    field = rows(512)
    half = rows(256)
    dma = pltpu.SemaphoreType.DMA
    out, cross = pl.pallas_call(
        kernel,
        out_shape=(
            jax.ShapeDtypeStruct((512, N), F32),
            jax.ShapeDtypeStruct((256, N), F32),
        ),
        in_specs=[hbm] * 4 + [smem] * 3 + [hbm] * 3,
        out_specs=(vmem, vmem),
        scratch_shapes=[
            field, half, pltpu.VMEM(square.shape, BF), pltpu.VMEM(dft.shape, F32), pltpu.VMEM(small.shape, BF),
            field, field, field, field, half, half, field, half, half,
            field, field, field, field, field, field, field, field,
            pltpu.VMEM((2, 256, 256), BF), pltpu.VMEM((2, 256, 256), BF),
            rows(N), half, field, half, field, half, half,
            dma((5,)), dma, dma((2,)), dma, dma((2,)), dma((4,)), dma((4,)),
            dma, dma, dma((4,)), dma, pltpu.SemaphoreType.REGULAR,
        ],
        compiler_params=pltpu.CompilerParams(
            collective_id=0, has_side_effects=True, vmem_limit_bytes=60 * 1024 * 1024
        ),
        name="window",
    )(
        orbitals.reshape(512, N),
        costate.reshape(512, N),
        potential.reshape(256, N),
        xc_kernel.reshape(256, N),
        vector_potential,
        kpoint_weight,
        occupation,
        jnp.asarray(square),
        jnp.asarray(dft),
        jnp.asarray(small),
    )
    return out.reshape(orbitals.shape), cross.reshape(potential.shape)


def solution(mesh):
    placed = (
        P("ka", None, None, "fft", None, None),
        P("ka", None, None, "fft", None, None),
        P("fft", None, None),
        P("fft", None, None),
        P(),
        P(),
        P(),
    )
    return jax.shard_map(
        local,
        mesh=mesh,
        in_specs=placed,
        out_specs=(P("ka", None, None, "fft", None, None), P("fft", None, None)),
        check_vma=False,
    )
```

```python
import functools
import math

import jax
import jax.numpy as jnp
import ml_dtypes
import numpy as np
from jax import lax
from jax.experimental import pallas as pl
from jax.experimental.pallas import tpu as pltpu
from jax.sharding import PartitionSpec as P

MESH = pl.DeviceIdType.MESH
N = 128
H = 64
STEPS = 2
SUB = 4
FAR = 52
FAR_OWNER = 74
KPTS = 4
spacing = 0.25
step_time = 0.6
SUB_TIME = step_time / SUB
UNIT = 2.0 * math.pi / (N * spacing)
BF = jnp.bfloat16
F32 = jnp.float32
PARTS = [(o, f, c) for o in range(2) for f in range(2) for c in range(2)]


def swap(index):
    return (index % 2) * 2 + index // 2


def slot_of(pair):
    return (pair // 32) * 32 + ((pair // 2) % 4) * 8 + (pair % 2) * 4 + (pair // 8) % 4


def plane_of(slot):
    return (slot // 32) * 32 + (slot % 4) * 8 + ((slot // 8) % 4) * 2 + (slot // 4) % 2


def split(matrix):
    high = matrix.astype(np.float32).astype(ml_dtypes.bfloat16)
    low = (matrix - high.astype(np.float64)).astype(np.float32).astype(ml_dtypes.bfloat16)
    return high, low


def constants():
    line = np.arange(N)
    signed = np.where(line < H, line, line - N)
    forward = np.exp(-2j * np.pi / N * ((line[:, None] * line[None, :]) % N))
    inverse = forward.conj().T / N
    order = np.array([c * N + 2 * q + f for f in range(2) for c in range(2) for q in range(H)])
    slots = [plane_of(q) for q in range(H)]
    order_x = np.array([c * N + 2 * q + f for f in range(2) for c in range(2) for q in slots])

    def stacked(matrix):
        return np.block([[matrix.real, -matrix.imag], [matrix.imag, matrix.real]])

    square = []
    for shift, side in ((0.25, "left"), (-0.25, "right")):
        wave = UNIT * (shift + signed)
        for sign in (1.0, -1.0):
            phase = np.exp(-1j * sign * 0.5 * SUB_TIME * wave * wave)
            full = stacked(inverse @ (phase[:, None] * forward))
            full = full[order][:, order] if side == "left" else full.T
            square += list(split(full))
    square += list(split(stacked(inverse)[order_x]))
    dft = stacked(forward)[:, order_x].astype(np.float32)

    real = np.zeros((N, N))
    real[0] = 1.0 / math.sqrt(N)
    real[N - 1] = np.cos(np.pi * line) / math.sqrt(N)
    for k in range(1, H):
        real[2 * k - 1] = math.sqrt(2.0 / N) * np.cos(2.0 * np.pi * (k * line % N) / N)
        real[2 * k] = math.sqrt(2.0 / N) * np.sin(2.0 * np.pi * (k * line % N) / N)
    pairs = np.array([2 * q + f for f in range(2) for q in range(H)])
    pairs_x = np.array([2 * q + f for f in range(2) for q in slots])
    small = []
    for matrix in (
        real[:, pairs], real[:, pairs].T, real.T, real, real[:, pairs_x], real[:, pairs_x].T,
    ):
        small += list(split(matrix))
    return np.stack(square), dft, np.stack(small)


AY, BZ, FINV = 0, 4, 8
R_IN, R_OUT, R_RIGHT, R_BACK, X_IN, X_OUT = 0, 2, 4, 6, 8, 10


def halves(value):
    high = value.astype(BF)
    return high, (value - high.astype(F32)).astype(BF)


def dot(a, b):
    return jnp.dot(a, b, preferred_element_type=F32)


def mul_left(high, low, value):
    vh, vl = halves(value)
    return dot(high, vh) + (dot(high, vl) + dot(low, vh))


def mul_right(value, high, low):
    vh, vl = halves(value)
    return dot(vh, high) + (dot(vl, high) + dot(vh, low))


def cat(values, axis):
    return jnp.concatenate(values, axis=axis)


def left(high, low, field):
    rows = [cat([field[0, f, c], field[1, f, c]], 1) for f in range(2) for c in range(2)]
    out = mul_left(high, low, cat(rows, 0))
    return {
        (o, f, c): out[(f * 2 + c) * H : (f * 2 + c + 1) * H, o * N : (o + 1) * N]
        for o, f, c in PARTS
    }


def right(high, low, field):
    rows = [cat([field[o, f, 0], field[o, f, 1]], 1) for o in range(2) for f in range(2)]
    out = mul_right(cat(rows, 0), high, low)
    return {
        (o, f, c): out[(o * 2 + f) * H : (o * 2 + f + 1) * H, c * N : (c + 1) * N]
        for o, f, c in PARTS
    }


def rotate(field, phase, sign):
    out = {}
    for o in range(2):
        for f in range(2):
            cosine, sine = phase[o, f, 0], sign * phase[o, f, 1]
            re, im = field[o, f, 0], field[o, f, 1]
            out[o, f, 0] = re * cosine + im * sine
            out[o, f, 1] = im * cosine - re * sine
    return out


def double(phase):
    out = {}
    for o in range(2):
        for f in range(2):
            cosine, sine = phase[o, f, 0], phase[o, f, 1]
            out[o, f, 0] = cosine * cosine - sine * sine
            out[o, f, 1] = 2.0 * cosine * sine
    return out


def read(ref):
    return {(o, f, c): ref[pl.ds((o * 4 + f * 2 + c) * H, H), :] for o, f, c in PARTS}


def write(ref, field):
    for o, f, c in PARTS:
        ref[pl.ds((o * 4 + f * 2 + c) * H, H), :] = field[o, f, c]


def read_tiles(ref):
    return {(o, f, c): ref[pl.ds(o * 4 + f * 2 + c, H, stride=8), :] for o, f, c in PARTS}


def write_tiles(ref, field):
    for o, f, c in PARTS:
        ref[pl.ds(f * 4 + o * 2 + c, H, stride=8), :] = field[o, f, c]


def read_planes(ref):
    return {(o, f, c): ref[pl.ds((c * 2 + o) * N + f, H, stride=2), :] for o, f, c in PARTS}


def phase_of(angles):
    out = {}
    for (o, f), angle in angles.items():
        out[o, f, 0] = jnp.cos(angle)
        out[o, f, 1] = jnp.sin(angle)
    return out


def plane_values(ref, factor):
    return {
        (o, f): factor * ref[pl.ds(o * N + f, H, stride=2), :] for o in range(2) for f in range(2)
    }


def column_values(ref, factor):
    return {
        (o, f): factor * ref[pl.ds(o * 2 + f, H, stride=4), :] for o in range(2) for f in range(2)
    }


def kernel(
    orb_in, cost, pot_in, xck, vec, weight, occupation, square_in, dft_in, small_in,
    out, cross_out,
    orb, pot, square, dft, small,
    send, recv0, recv1, recv_last, column_send, column_recv, cost_recv, pot_recv, xck_recv,
    orig_phase, plane_one, plane_two, col_two, cur, psi_one, psi, adj, first, second,
    coulomb, h_send, h_recv, b_send, b_recv, cross_stage, cross_recv,
    load_sem, send_sem, recv_sem, last_sem, phase_sem, move_send, move_recv,
    h_send_sem, h_recv_sem, b_send_sem, b_recv_sem, known,
):
    ka = lax.axis_index("ka")
    fft = lax.axis_index("fft")
    block = fft // 16
    member = (fft % 16) * 4 + ka
    ident = fft * 4 + ka
    point = swap(block)
    goal = swap(ka)
    home = block == goal
    slot = slot_of(fft)
    plane = plane_of(member)
    stay = jnp.logical_and(home, member == slot)

    def place(p):
        return (jnp.bitwise_and(p, 3), lax.shift_right_logical(p, 2))

    def spread(start, count, own, unroll=4):
        lax.fori_loop(0, own, lambda d, c: start(d), 0, unroll=unroll)
        lax.fori_loop(own + 1, count, lambda d, c: start(d), 0, unroll=count - own - 1)

    def remote(src, dst, ss, rs, device):
        return pltpu.make_async_remote_copy(
            src_ref=src, dst_ref=dst, send_sem=ss, recv_sem=rs, device_id=device, device_id_type=MESH
        )

    def wait_rows(ref, rows, sem):
        part = ref.at[pl.ds(0, rows)]
        pltpu.make_async_copy(part, part, sem).wait()

    def tile(ref, index, rows=8):
        return ref.at[pl.ds(pl.multiple_of(index * rows, rows), rows)]

    loads = [
        pltpu.make_async_copy(src, dst, load_sem.at[index])
        for index, (src, dst) in enumerate(
            ((pot_in, pot), (orb_in, orb), (square_in, square), (dft_in, dft), (small_in, small))
        )
    ]
    for load in loads:
        load.start()

    barrier = pltpu.get_barrier_semaphore()

    def greet(d, carry):
        peer = jnp.bitwise_xor(fft, d)

        @pl.when(jnp.logical_not(jnp.logical_and(home, d == 0)))
        def _():
            pl.semaphore_signal(barrier, inc=1, device_id=(point, peer), device_id_type=MESH)

        return carry

    lax.fori_loop(0, 64, greet, 0)

    loads[0].wait()
    for o in range(2):
        for f in range(2):
            column_send[pl.ds(f * 2 + o, H, stride=4), :] = pot[pl.ds(o * N + f, H, stride=2), :]
    phase = phase_of(plane_values(pot, 0.5 * SUB_TIME))
    write(orig_phase, phase)
    loads[1].wait()
    field = rotate(read_planes(orb), phase, 1.0)
    loads[2].wait()
    field = right(square[BZ], square[BZ + 1], field)
    field = left(square[AY], square[AY + 1], field)
    write_tiles(send, field)

    @pl.when(home)
    def _():
        pl.semaphore_wait(barrier, 63)

    @pl.when(jnp.logical_not(home))
    def _():
        pl.semaphore_wait(barrier, 64)

    def start_first(src, dst, rows, ss, rs):
        def start(d, carry):
            p = jnp.bitwise_xor(member, jnp.bitwise_xor(d, FAR))
            own = jnp.logical_and(home, d == FAR)

            @pl.when(jnp.logical_not(own))
            def _():
                device = place(goal * 64 + p)
                remote(tile(src, p, rows), tile(dst, slot, rows), ss, rs, device).start()

            @pl.when(own)
            def _():
                pltpu.make_async_copy(tile(src, p, rows), tile(dst, slot, rows), rs).start()

            return carry

        lax.fori_loop(0, 64, start, 0)

    start_first(send, recv0, 8, send_sem, recv_sem.at[0])
    start_first(column_send, column_recv, 4, phase_sem.at[0], phase_sem.at[1])

    def start_move(src, dst, index):
        @pl.when(stay)
        def _():
            pltpu.make_async_copy(src, dst, move_recv.at[index]).start()

        @pl.when(jnp.logical_not(stay))
        def _():
            device = place(goal * 64 + slot)
            remote(src, dst, move_send.at[index], move_recv.at[index], device).start()

    def wait_move(src, dst, index):
        pltpu.make_async_copy(dst, dst, move_recv.at[index]).wait()

        @pl.when(jnp.logical_not(stay))
        def _():
            pltpu.make_async_copy(src, src, move_send.at[index]).wait()

    column = fft * 2 + ka // 2
    owner = ka % 2 == 0
    unit_y = (UNIT * ((column + 1) // 2)).astype(F32)
    along_x = (lax.broadcasted_iota(jnp.int32, (N, N), 0) + 1) // 2
    along_z = (lax.broadcasted_iota(jnp.int32, (N, N), 1) + 1) // 2
    wave_x = UNIT * along_x.astype(F32)
    wave_z = UNIT * along_z.astype(F32)
    g_squared = wave_x * wave_x + unit_y * unit_y + wave_z * wave_z
    positive = g_squared > 0
    coulomb[...] = jnp.where(positive, 4.0 * math.pi / jnp.where(positive, g_squared, 1.0), 0.0)

    shift_x = UNIT * ((point.astype(F32) + 0.5) / KPTS - 0.5)

    def build(target, sub_index, sign):
        mode = lax.broadcasted_iota(jnp.int32, (N, N), 0)
        mode = jnp.where(mode < H, mode, mode - N).astype(F32)
        wave = shift_x + UNIT * mode + vec[sub_index]
        angle = (0.5 * SUB_TIME) * (wave * wave)
        cosine, sine = jnp.cos(angle), sign * jnp.sin(angle)
        cosine, sine = cat([cosine, cosine], 1), cat([sine, sine], 1)
        re, im = dft[0:N, :], dft[N : 2 * N, :]
        turned = cat([re * cosine + im * sine, im * cosine - re * sine], 0)
        made = mul_left(square[FINV], square[FINV + 1], turned)
        high, low = halves(made)
        target[0] = high
        target[1] = low

    def start_inside(target, sem):
        def start(d):
            p = jnp.bitwise_xor(member, jnp.bitwise_xor(d, FAR))
            remote(
                tile(send, p), tile(target, member), send_sem, sem, place(block * 64 + p)
            ).start()
            return 0

        spread(start, 64, FAR)
        pltpu.make_async_copy(tile(send, member), tile(target, member), sem).start()

    def move_quarter(i, part):
        @pl.when(jnp.logical_or(i == 1, i == 2))
        def _():
            quarter = 2 * (i - 1) + part
            start_move(tile(cost, quarter, N), tile(cost_recv, quarter, N), 2)

        @pl.when(i == 3 - 3 * part)
        def _():
            start_move(tile(xck, 1 - part, N), tile(xck_recv, 1 - part, N), 1)

    def columns(i, sign):
        forward = i < 4

        @pl.when(i == 0)
        def _():
            loads[3].wait()
            loads[4].wait()

        build(first, jnp.where(forward, 2 * i, 15 - 2 * i), sign)
        build(second, jnp.where(forward, 2 * i + 1, 14 - 2 * i), sign)
        wait_rows(recv0, 512, recv_sem.at[0])
        move_quarter(i, 0)

        @pl.when(jnp.logical_and(i == 0, jnp.logical_not(home)))
        def _():
            wait_rows(send, 512, send_sem)

        @pl.when(jnp.logical_or(i > 0, home))
        def _():
            wait_rows(send, 504, send_sem)

        @pl.when(i == 0)
        def _():
            start_move(pot_in, pot_recv, 0)
            wait_rows(column_recv, 256, phase_sem.at[1])
            write(col_two, phase_of(column_values(column_recv, SUB_TIME)))

            @pl.when(ka == 0)
            def _():
                for step in range(1, 4):
                    other = (block + step) % 4
                    pl.semaphore_signal(
                        known, inc=1, device_id=(point, other * 16 + fft % 16), device_id_type=MESH
                    )

        field = left(first[0], first[1], read_tiles(recv0))
        field = rotate(field, read(col_two), sign)
        field = left(second[0], second[1], field)
        back = jnp.where(forward, BZ, BZ + 2)
        field = right(square[back], square[back + 1], field)
        write_tiles(send, field)

    def response(last):
        wave, other = read(psi), read(adj)
        total = weight[0] + weight[1] + weight[2] + weight[3]
        share = weight[point].astype(F32) / total.astype(F32)
        factor = 2.0 * share * (occupation[0].astype(F32) / 100.0)
        own = {
            (o, f): factor * (other[o, f, 0] * wave[o, f, 0] + other[o, f, 1] * wave[o, f, 1])
            for o in range(2)
            for f in range(2)
        }
        dense = cat([cat([own[0, f], own[1, f]], 1) for f in range(2)], 0)
        dense = mul_left(small[R_IN], small[R_IN + 1], dense)
        dense = mul_right(
            cat([dense[:, 0:N], dense[:, N : 2 * N]], 0), small[R_RIGHT], small[R_RIGHT + 1]
        )
        for o in range(2):
            h_send[pl.ds(o, N, stride=2), :] = dense[o * N : (o + 1) * N]

        def send_dense(to):
            device = (jnp.bitwise_and(to, 1) * 2, lax.shift_right_logical(to, 1))
            remote(
                tile(h_send, to, 2), tile(h_recv, ident, 2), h_send_sem, h_recv_sem, device
            ).start()

        def start_dense(d):
            send_dense(jnp.bitwise_xor(column, jnp.bitwise_xor(d, FAR_OWNER)))
            return 0

        lax.fori_loop(0, FAR_OWNER, lambda d, c: start_dense(d), 0, unroll=2)
        lax.fori_loop(FAR_OWNER + 1, N, lambda d, c: start_dense(d), 0)

        @pl.when(owner)
        def _():
            pltpu.make_async_copy(
                tile(h_send, column, 2), tile(h_recv, ident, 2), h_recv_sem
            ).start()

        @pl.when(jnp.logical_not(owner))
        def _():
            send_dense(column)

        @pl.when(owner)
        def _():
            wait_rows(h_recv, 512, h_recv_sem)
            summed = []
            for f in range(2):
                terms = [h_recv[pl.ds(k * N + f, H, stride=2), :] for k in range(4)]
                summed.append((terms[0] + terms[1]) + (terms[2] + terms[3]))
            line = mul_left(small[X_IN], small[X_IN + 1], cat(summed, 0)) * coulomb[...]
            line = mul_left(small[X_OUT], small[X_OUT + 1], line)
            for f in range(2):
                b_send[pl.ds(f, H, stride=4), :] = line[f * H : (f + 1) * H]
                b_send[pl.ds(2 + f, H, stride=4), :] = summed[f]
            for group in (2, 3, 1, 0):
                there = jnp.bitwise_and(block + group, 3) * 64

                def start_back(d, group=group, there=there):
                    p = jnp.bitwise_xor(member, jnp.bitwise_xor(d, FAR))
                    remote(
                        tile(b_send, p, 4),
                        tile(b_recv, column, 4),
                        b_send_sem.at[group],
                        b_recv_sem,
                        place(there + p),
                    ).start()
                    return 0

                if group:
                    lax.fori_loop(0, 64, lambda d, c: start_back(d), 0, unroll=4)
                else:
                    spread(start_back, 64, FAR)
            pltpu.make_async_copy(
                tile(b_send, member, 4), tile(b_recv, column, 4), b_recv_sem
            ).start()

        @pl.when(jnp.logical_not(last))
        def _():
            wait_move(xck, xck_recv, 1)

        wait_rows(b_recv, 512, b_recv_sem)
        parts = [b_recv[pl.ds(r, N, stride=4), :] for r in range(4)]
        parts = mul_right(cat(parts, 0), small[R_BACK], small[R_BACK + 1])
        parts = cat([parts[r * N : (r + 1) * N] for r in range(4)], 1)
        parts = mul_left(small[R_OUT], small[R_OUT + 1], parts)
        for o in range(2):
            for f in range(2):
                rows = slice(f * H, (f + 1) * H)
                hartree = parts[rows, o * N : (o + 1) * N]
                density = parts[rows, (2 + o) * N : (3 + o) * N]
                cross = hartree + xck_recv[pl.ds(o * N + f, H, stride=2), :] * density
                cross_stage[pl.ds(o * N + f, H, stride=2), :] = cross
                base = (o * 4 + f * 2) * H
                cur[pl.ds(base, H), :] = other[o, f, 0] + step_time * cross * wave[o, f, 1]
                cur[pl.ds(base + H, H), :] = other[o, f, 1] - step_time * cross * wave[o, f, 0]

        @pl.when(owner)
        def _():
            wait_rows(h_send, 254, h_send_sem)
            wait_rows(b_send, 252, b_send_sem.at[0])
            for group in range(1, 4):
                wait_rows(b_send, 256, b_send_sem.at[group])

        @pl.when(jnp.logical_not(owner))
        def _():
            wait_rows(h_send, 256, h_send_sem)

        @pl.when(last)
        def _():
            @pl.when(stay)
            def _():
                pltpu.make_async_copy(cross_stage, cross_recv, move_recv.at[3]).start()

            @pl.when(jnp.logical_not(stay))
            def _():
                remote(
                    cross_stage, cross_recv, move_send.at[3], move_recv.at[3], (point, plane)
                ).start()

    def pair(i, carry):
        sign = jnp.where(i < 4, 1.0, -1.0).astype(F32)
        columns(i, sign)
        start_inside(recv1, recv_sem.at[1])

        @pl.when(i == 0)
        def _():
            wait_move(pot_in, pot_recv, 0)
            phase = phase_of(plane_values(pot_recv, 0.5 * SUB_TIME))
            write(plane_one, phase)
            write(plane_two, double(phase))


        wait_rows(recv1, 512, recv_sem.at[1])
        move_quarter(i, 1)
        wait_rows(send, 504, send_sem)
        turn = jnp.where(i < 4, AY, AY + 2)
        field = left(square[turn], square[turn + 1], read_tiles(recv1))

        @pl.when(i % 2 == 0)
        def _():
            write(cur, rotate(field, read(plane_two), sign))

        @pl.when(i % 2 == 1)
        def _():
            write(cur, rotate(field, read(plane_one), sign))

        @pl.when(i == 1)
        def _():
            psi_one[...] = cur[...]

        @pl.when(i == 3)
        def _():
            wait_move(cost, cost_recv, 2)
            psi[...] = cur[...]
            write(adj, read_planes(cost_recv))

        @pl.when(i == 5)
        def _():
            psi[...] = psi_one[...]
            adj[...] = cur[...]

        @pl.when(jnp.logical_or(i == 3, i == 5))
        def _():
            response(i == 5)

        sign_next = jnp.where(i < 3, 1.0, -1.0).astype(F32)

        @pl.when(i % 2 == 1)
        def _():
            write(cur, rotate(read(cur), read(plane_one), sign_next))

        turn = jnp.where(i < 3, AY, AY + 2)
        back = jnp.where(i < 3, BZ, BZ + 2)
        field = right(square[back], square[back + 1], read(cur))
        field = left(square[turn], square[turn + 1], field)
        write_tiles(send, field)

        @pl.when(jnp.logical_and(i == 0, jnp.logical_not(home)))
        def _():
            pl.semaphore_wait(known, 1)

        start_inside(recv0, recv_sem.at[0])
        return carry

    lax.fori_loop(0, 7, pair, 0)

    columns(jnp.int32(7), jnp.float32(-1.0))

    def start_last(d, carry):
        q = jnp.bitwise_xor(fft, d)
        own = jnp.logical_and(home, d == 0)

        @pl.when(jnp.logical_not(own))
        def _():
            remote(
                tile(send, slot_of(q)), tile(recv_last, member), send_sem, last_sem, (point, q)
            ).start()

        @pl.when(own)
        def _():
            pltpu.make_async_copy(
                tile(send, slot_of(q)), tile(recv_last, member), last_sem
            ).start()

        return carry

    lax.fori_loop(0, 64, start_last, 0)

    pltpu.make_async_copy(cross_recv, cross_recv, move_recv.at[3]).wait()
    cross_out[...] = cross_recv[...]

    @pl.when(jnp.logical_not(stay))
    def _():
        pltpu.make_async_copy(cross_stage, cross_stage, move_send.at[3]).wait()

    wait_rows(recv_last, 512, last_sem)
    field = left(square[AY + 2], square[AY + 3], read_tiles(recv_last))
    field = rotate(field, read(orig_phase), -1.0)
    for o, f, c in PARTS:
        out[pl.ds((c * 2 + o) * N + f, H, stride=2), :] = field[o, f, c]

    @pl.when(home)
    def _():
        wait_rows(send, 504, send_sem)
        wait_rows(column_send, 252, phase_sem.at[0])

    @pl.when(jnp.logical_not(home))
    def _():
        wait_rows(send, 512, send_sem)
        wait_rows(column_send, 256, phase_sem.at[0])


def local(orbitals, costate, potential, xc_kernel, vector_potential, kpoint_weight, occupation):
    square, dft, small = constants()
    vmem = pl.BlockSpec(memory_space=pltpu.VMEM)
    smem = pl.BlockSpec(memory_space=pltpu.SMEM)
    hbm = pl.BlockSpec(memory_space=pltpu.HBM)

    def rows(count):
        return pltpu.VMEM((count, N), F32)

    field = rows(512)
    half = rows(256)
    dma = pltpu.SemaphoreType.DMA
    out, cross = pl.pallas_call(
        kernel,
        out_shape=(
            jax.ShapeDtypeStruct((512, N), F32),
            jax.ShapeDtypeStruct((256, N), F32),
        ),
        in_specs=[hbm] * 4 + [smem] * 3 + [hbm] * 3,
        out_specs=(vmem, vmem),
        scratch_shapes=[
            field, half, pltpu.VMEM(square.shape, BF), pltpu.VMEM(dft.shape, F32), pltpu.VMEM(small.shape, BF),
            field, field, field, field, half, half, field, half, half,
            field, field, field, field, field, field, field, field,
            pltpu.VMEM((2, 256, 256), BF), pltpu.VMEM((2, 256, 256), BF),
            rows(N), half, field, half, field, half, half,
            dma((5,)), dma, dma((2,)), dma, dma((2,)), dma((4,)), dma((4,)),
            dma, dma, dma((4,)), dma, pltpu.SemaphoreType.REGULAR,
        ],
        compiler_params=pltpu.CompilerParams(
            collective_id=0, has_side_effects=True, vmem_limit_bytes=60 * 1024 * 1024
        ),
        name="window",
    )(
        orbitals.reshape(512, N),
        costate.reshape(512, N),
        potential.reshape(256, N),
        xc_kernel.reshape(256, N),
        vector_potential,
        kpoint_weight,
        occupation,
        jnp.asarray(square),
        jnp.asarray(dft),
        jnp.asarray(small),
    )
    return out.reshape(orbitals.shape), cross.reshape(potential.shape)


def solution(mesh):
    placed = (
        P("ka", None, None, "fft", None, None),
        P("ka", None, None, "fft", None, None),
        P("fft", None, None),
        P("fft", None, None),
        P(),
        P(),
        P(),
    )
    return jax.shard_map(
        local,
        mesh=mesh,
        in_specs=placed,
        out_specs=(P("ka", None, None, "fft", None, None), P("fft", None, None)),
        check_vma=False,
    )
```

```python
import functools
import math

import jax
import jax.numpy as jnp
import ml_dtypes
import numpy as np
from jax import lax
from jax.experimental import pallas as pl
from jax.experimental.pallas import tpu as pltpu
from jax.sharding import PartitionSpec as P

MESH = pl.DeviceIdType.MESH
N = 128
H = 64
STEPS = 2
SUB = 4
FAR = 52
FAR_OWNER = 74
FAR_PLANE = 37
KPTS = 4
spacing = 0.25
step_time = 0.6
SUB_TIME = step_time / SUB
UNIT = 2.0 * math.pi / (N * spacing)
BF = jnp.bfloat16
F32 = jnp.float32
PARTS = [(o, f, c) for o in range(2) for f in range(2) for c in range(2)]


def swap(index):
    return (index % 2) * 2 + index // 2


def slot_of(pair):
    return (pair // 32) * 32 + ((pair // 2) % 4) * 8 + (pair % 2) * 4 + (pair // 8) % 4


def plane_of(slot):
    return (slot // 32) * 32 + (slot % 4) * 8 + ((slot // 8) % 4) * 2 + (slot // 4) % 2


def split(matrix):
    high = matrix.astype(np.float32).astype(ml_dtypes.bfloat16)
    low = (matrix - high.astype(np.float64)).astype(np.float32).astype(ml_dtypes.bfloat16)
    return high, low


def constants():
    line = np.arange(N)
    signed = np.where(line < H, line, line - N)
    forward = np.exp(-2j * np.pi / N * ((line[:, None] * line[None, :]) % N))
    inverse = forward.conj().T / N
    order = np.array([c * N + 2 * q + f for f in range(2) for c in range(2) for q in range(H)])
    slots = [plane_of(q) for q in range(H)]
    order_x = np.array([c * N + 2 * q + f for f in range(2) for c in range(2) for q in slots])

    def stacked(matrix):
        return np.block([[matrix.real, -matrix.imag], [matrix.imag, matrix.real]])

    square = []
    for shift, side in ((0.25, "left"), (-0.25, "right")):
        wave = UNIT * (shift + signed)
        for sign in (1.0, -1.0):
            phase = np.exp(-1j * sign * 0.5 * SUB_TIME * wave * wave)
            full = stacked(inverse @ (phase[:, None] * forward))
            full = full[order][:, order] if side == "left" else full.T
            square += list(split(full))
    square += list(split(stacked(inverse)[order_x]))
    dft = stacked(forward)[:, order_x].astype(np.float32)

    real = np.zeros((N, N))
    real[0] = 1.0 / math.sqrt(N)
    real[N - 1] = np.cos(np.pi * line) / math.sqrt(N)
    for k in range(1, H):
        real[2 * k - 1] = math.sqrt(2.0 / N) * np.cos(2.0 * np.pi * (k * line % N) / N)
        real[2 * k] = math.sqrt(2.0 / N) * np.sin(2.0 * np.pi * (k * line % N) / N)
    pairs = np.array([2 * q + f for f in range(2) for q in range(H)])
    pairs_x = np.array([2 * q + f for f in range(2) for q in slots])
    small = []
    for matrix in (
        real[:, pairs], real[:, pairs].T, real.T, real, real[:, pairs_x], real[:, pairs_x].T,
    ):
        small += list(split(matrix))
    return np.stack(square), dft, np.stack(small)


AY, BZ, FINV = 0, 4, 8
R_IN, R_OUT, R_RIGHT, R_BACK, X_IN, X_OUT = 0, 2, 4, 6, 8, 10


def halves(value):
    high = value.astype(BF)
    return high, (value - high.astype(F32)).astype(BF)


def dot(a, b):
    return jnp.dot(a, b, preferred_element_type=F32)


def mul_left(high, low, value):
    vh, vl = halves(value)
    return dot(high, vh) + (dot(high, vl) + dot(low, vh))


def mul_right(value, high, low):
    vh, vl = halves(value)
    return dot(vh, high) + (dot(vl, high) + dot(vh, low))


def cat(values, axis):
    return jnp.concatenate(values, axis=axis)


def left(high, low, field):
    rows = [cat([field[0, f, c], field[1, f, c]], 1) for f in range(2) for c in range(2)]
    out = mul_left(high, low, cat(rows, 0))
    return {
        (o, f, c): out[(f * 2 + c) * H : (f * 2 + c + 1) * H, o * N : (o + 1) * N]
        for o, f, c in PARTS
    }


def right(high, low, field):
    rows = [cat([field[o, f, 0], field[o, f, 1]], 1) for o in range(2) for f in range(2)]
    out = mul_right(cat(rows, 0), high, low)
    return {
        (o, f, c): out[(o * 2 + f) * H : (o * 2 + f + 1) * H, c * N : (c + 1) * N]
        for o, f, c in PARTS
    }


def rotate(field, phase, sign):
    out = {}
    for o in range(2):
        for f in range(2):
            cosine, sine = phase[o, f, 0], sign * phase[o, f, 1]
            re, im = field[o, f, 0], field[o, f, 1]
            out[o, f, 0] = re * cosine + im * sine
            out[o, f, 1] = im * cosine - re * sine
    return out


def double(phase):
    out = {}
    for o in range(2):
        for f in range(2):
            cosine, sine = phase[o, f, 0], phase[o, f, 1]
            out[o, f, 0] = cosine * cosine - sine * sine
            out[o, f, 1] = 2.0 * cosine * sine
    return out


def read(ref):
    return {(o, f, c): ref[pl.ds((o * 4 + f * 2 + c) * H, H), :] for o, f, c in PARTS}


def write(ref, field):
    for o, f, c in PARTS:
        ref[pl.ds((o * 4 + f * 2 + c) * H, H), :] = field[o, f, c]


def read_tiles(ref):
    return {(o, f, c): ref[pl.ds(o * 4 + f * 2 + c, H, stride=8), :] for o, f, c in PARTS}


def write_tiles(ref, field):
    for o, f, c in PARTS:
        ref[pl.ds(f * 4 + o * 2 + c, H, stride=8), :] = field[o, f, c]


def read_planes(ref):
    return {(o, f, c): ref[pl.ds((c * 2 + o) * N + f, H, stride=2), :] for o, f, c in PARTS}


def phase_of(angles):
    out = {}
    for (o, f), angle in angles.items():
        out[o, f, 0] = jnp.cos(angle)
        out[o, f, 1] = jnp.sin(angle)
    return out


def plane_values(ref, factor):
    return {
        (o, f): factor * ref[pl.ds(o * N + f, H, stride=2), :] for o in range(2) for f in range(2)
    }


def tile_values(ref, factor, step_own, step_far):
    return {
        (o, f): factor * ref[pl.ds(o * step_own + f * step_far, H, stride=4), :]
        for o in range(2)
        for f in range(2)
    }


def kernel(
    orb_in, cost, pot_in, xck, vec, weight, occupation, square_in, dft_in, small_in,
    out, cross_out,
    orb, pot, square, dft, small,
    send, recv0, recv1, recv_last, column_send, column_recv, cost_recv, pot_recv, xck_recv,
    orig_phase, plane_one, plane_two, col_two, cur, psi_one, psi, adj, first, second,
    coulomb, h_send, h_recv, b_send, b_recv, cross_stage, cross_recv,
    load_sem, send_sem, recv_sem, last_sem, phase_sem, move_send, move_recv,
    h_send_sem, h_recv_sem, b_send_sem, b_recv_sem, known,
):
    ka = lax.axis_index("ka")
    fft = lax.axis_index("fft")
    block = fft // 16
    member = (fft % 16) * 4 + ka
    ident = fft * 4 + ka
    point = swap(block)
    goal = swap(ka)
    home = block == goal
    slot = slot_of(fft)
    plane = plane_of(member)
    stay = jnp.logical_and(home, member == slot)

    def place(p):
        return (jnp.bitwise_and(p, 3), lax.shift_right_logical(p, 2))

    def spread(start, count, own, unroll=4):
        lax.fori_loop(0, own, lambda d, c: start(d), 0, unroll=unroll)
        lax.fori_loop(own + 1, count, lambda d, c: start(d), 0, unroll=count - own - 1)

    def remote(src, dst, ss, rs, device):
        return pltpu.make_async_remote_copy(
            src_ref=src, dst_ref=dst, send_sem=ss, recv_sem=rs, device_id=device, device_id_type=MESH
        )

    def wait_rows(ref, rows, sem):
        part = ref.at[pl.ds(0, rows)]
        pltpu.make_async_copy(part, part, sem).wait()

    def tile(ref, index, rows=8):
        return ref.at[pl.ds(pl.multiple_of(index * rows, rows), rows)]

    loads = [
        pltpu.make_async_copy(src, dst, load_sem.at[index])
        for index, (src, dst) in enumerate(
            ((pot_in, pot), (orb_in, orb), (square_in, square), (dft_in, dft), (small_in, small))
        )
    ]
    for load in loads:
        load.start()

    barrier = pltpu.get_barrier_semaphore()

    def greet(d, carry):
        peer = jnp.bitwise_xor(fft, d)

        @pl.when(jnp.logical_not(jnp.logical_and(home, d == 0)))
        def _():
            pl.semaphore_signal(barrier, inc=1, device_id=(point, peer), device_id_type=MESH)

        return carry

    lax.fori_loop(0, 64, greet, 0)

    loads[0].wait()
    for o in range(2):
        for f in range(2):
            column_send[pl.ds(f * 2 + o, H, stride=4), :] = pot[pl.ds(o * N + f, H, stride=2), :]
    phase = phase_of(plane_values(pot, 0.5 * SUB_TIME))
    write(orig_phase, phase)
    loads[1].wait()
    field = rotate(read_planes(orb), phase, 1.0)
    loads[2].wait()
    field = right(square[BZ], square[BZ + 1], field)
    field = left(square[AY], square[AY + 1], field)
    write_tiles(send, field)

    @pl.when(home)
    def _():
        pl.semaphore_wait(barrier, 63)

    @pl.when(jnp.logical_not(home))
    def _():
        pl.semaphore_wait(barrier, 64)

    def start_first(src, dst, rows, ss, rs):
        def start(d, carry):
            p = jnp.bitwise_xor(member, jnp.bitwise_xor(d, FAR))
            own = jnp.logical_and(home, d == FAR)

            @pl.when(jnp.logical_not(own))
            def _():
                device = place(goal * 64 + p)
                remote(tile(src, p, rows), tile(dst, slot, rows), ss, rs, device).start()

            @pl.when(own)
            def _():
                pltpu.make_async_copy(tile(src, p, rows), tile(dst, slot, rows), rs).start()

            return carry

        lax.fori_loop(0, 64, start, 0)

    start_first(send, recv0, 8, send_sem, recv_sem.at[0])
    start_first(column_send, column_recv, 4, phase_sem.at[0], phase_sem.at[1])

    def start_move(src, dst, index):
        @pl.when(stay)
        def _():
            pltpu.make_async_copy(src, dst, move_recv.at[index]).start()

        @pl.when(jnp.logical_not(stay))
        def _():
            device = place(goal * 64 + slot)
            remote(src, dst, move_send.at[index], move_recv.at[index], device).start()

    def wait_move(src, dst, index):
        pltpu.make_async_copy(dst, dst, move_recv.at[index]).wait()

        @pl.when(jnp.logical_not(stay))
        def _():
            pltpu.make_async_copy(src, src, move_send.at[index]).wait()

    column = fft * 2 + ka // 2
    owner = ka % 2 == 0
    unit_y = (UNIT * ((column + 1) // 2)).astype(F32)
    along_x = (lax.broadcasted_iota(jnp.int32, (N, N), 0) + 1) // 2
    along_z = (lax.broadcasted_iota(jnp.int32, (N, N), 1) + 1) // 2
    wave_x = UNIT * along_x.astype(F32)
    wave_z = UNIT * along_z.astype(F32)
    g_squared = wave_x * wave_x + unit_y * unit_y + wave_z * wave_z
    positive = g_squared > 0
    coulomb[...] = jnp.where(positive, 4.0 * math.pi / jnp.where(positive, g_squared, 1.0), 0.0)

    shift_x = UNIT * ((point.astype(F32) + 0.5) / KPTS - 0.5)

    def build(target, sub_index, sign):
        mode = lax.broadcasted_iota(jnp.int32, (N, N), 0)
        mode = jnp.where(mode < H, mode, mode - N).astype(F32)
        wave = shift_x + UNIT * mode + vec[sub_index]
        angle = (0.5 * SUB_TIME) * (wave * wave)
        cosine, sine = jnp.cos(angle), sign * jnp.sin(angle)
        cosine, sine = cat([cosine, cosine], 1), cat([sine, sine], 1)
        re, im = dft[0:N, :], dft[N : 2 * N, :]
        turned = cat([re * cosine + im * sine, im * cosine - re * sine], 0)
        made = mul_left(square[FINV], square[FINV + 1], turned)
        high, low = halves(made)
        target[0] = high
        target[1] = low

    def start_inside(target, sem):
        def start(d):
            p = jnp.bitwise_xor(member, jnp.bitwise_xor(d, FAR))
            remote(
                tile(send, p), tile(target, member), send_sem, sem, place(block * 64 + p)
            ).start()
            return 0

        spread(start, 64, FAR)
        pltpu.make_async_copy(tile(send, member), tile(target, member), sem).start()

    def move_quarter(i, part):
        @pl.when(jnp.logical_or(i == 1, i == 2))
        def _():
            quarter = 2 * (i - 1) + part
            start_move(tile(cost, quarter, N), tile(cost_recv, quarter, N), 2)

        @pl.when(i == 3 - 3 * part)
        def _():
            start_move(tile(xck, 1 - part, N), tile(xck_recv, 1 - part, N), 1)

        @pl.when(i == 6)
        def _():
            src, dst = tile(cross_stage, part, N), tile(cross_recv, part, N)

            @pl.when(stay)
            def _():
                pltpu.make_async_copy(src, dst, move_recv.at[3]).start()

            @pl.when(jnp.logical_not(stay))
            def _():
                remote(src, dst, move_send.at[3], move_recv.at[3], (point, plane)).start()

    def columns(i, sign):
        forward = i < 4

        @pl.when(i == 0)
        def _():
            loads[3].wait()
            loads[4].wait()

        build(first, jnp.where(forward, 2 * i, 15 - 2 * i), sign)
        build(second, jnp.where(forward, 2 * i + 1, 14 - 2 * i), sign)
        wait_rows(recv0, 512, recv_sem.at[0])
        move_quarter(i, 0)

        @pl.when(jnp.logical_and(i == 0, jnp.logical_not(home)))
        def _():
            wait_rows(send, 512, send_sem)

        @pl.when(jnp.logical_or(i > 0, home))
        def _():
            wait_rows(send, 504, send_sem)

        @pl.when(i == 0)
        def _():
            wait_rows(column_recv, 256, phase_sem.at[1])

            def start_planes(d):
                p = jnp.bitwise_xor(member, jnp.bitwise_xor(d, FAR))
                remote(
                    tile(column_recv, p, 4),
                    tile(pot_recv, member, 4),
                    move_send.at[0],
                    move_recv.at[0],
                    place(block * 64 + p),
                ).start()
                return 0

            spread(start_planes, 64, FAR)
            pltpu.make_async_copy(
                tile(column_recv, member, 4), tile(pot_recv, member, 4), move_recv.at[0]
            ).start()
            write(col_two, phase_of(tile_values(column_recv, SUB_TIME, 2, 1)))

            @pl.when(ka == 0)
            def _():
                for step in range(1, 4):
                    other = (block + step) % 4
                    pl.semaphore_signal(
                        known, inc=1, device_id=(point, other * 16 + fft % 16), device_id_type=MESH
                    )

        field = left(first[0], first[1], read_tiles(recv0))
        field = rotate(field, read(col_two), sign)
        field = left(second[0], second[1], field)
        back = jnp.where(forward, BZ, BZ + 2)
        field = right(square[back], square[back + 1], field)
        write_tiles(send, field)

    def response(first_time):
        wave, other = read(psi), read(adj)
        total = weight[0] + weight[1] + weight[2] + weight[3]
        share = weight[point].astype(F32) / total.astype(F32)
        factor = 2.0 * share * (occupation[0].astype(F32) / 100.0)
        own = {
            (o, f): factor * (other[o, f, 0] * wave[o, f, 0] + other[o, f, 1] * wave[o, f, 1])
            for o in range(2)
            for f in range(2)
        }
        dense = cat([cat([own[0, f], own[1, f]], 1) for f in range(2)], 0)
        dense = mul_left(small[R_IN], small[R_IN + 1], dense)
        dense = mul_right(
            cat([dense[:, 0:N], dense[:, N : 2 * N]], 0), small[R_RIGHT], small[R_RIGHT + 1]
        )
        for o in range(2):
            h_send[pl.ds(o, N, stride=2), :] = dense[o * N : (o + 1) * N]

        def send_dense(to):
            device = (jnp.bitwise_and(to, 1) * 2, lax.shift_right_logical(to, 1))
            remote(
                tile(h_send, to, 2), tile(h_recv, ident, 2), h_send_sem, h_recv_sem, device
            ).start()

        def start_dense(d):
            send_dense(jnp.bitwise_xor(column, jnp.bitwise_xor(d, FAR_OWNER)))
            return 0

        lax.fori_loop(0, FAR_OWNER, lambda d, c: start_dense(d), 0, unroll=2)
        lax.fori_loop(FAR_OWNER + 1, N, lambda d, c: start_dense(d), 0)

        @pl.when(owner)
        def _():
            pltpu.make_async_copy(
                tile(h_send, column, 2), tile(h_recv, ident, 2), h_recv_sem
            ).start()

        @pl.when(jnp.logical_not(owner))
        def _():
            send_dense(column)

        @pl.when(owner)
        def _():
            wait_rows(h_recv, 512, h_recv_sem)
            summed = []
            for f in range(2):
                terms = [h_recv[pl.ds(k * N + f, H, stride=2), :] for k in range(4)]
                summed.append((terms[0] + terms[1]) + (terms[2] + terms[3]))
            line = mul_left(small[X_IN], small[X_IN + 1], cat(summed, 0)) * coulomb[...]
            line = mul_left(small[X_OUT], small[X_OUT + 1], line)
            for f in range(2):
                b_send[pl.ds(f, H, stride=4), :] = line[f * H : (f + 1) * H]
                b_send[pl.ds(2 + f, H, stride=4), :] = summed[f]
            for group in (2, 3, 1, 0):
                there = jnp.bitwise_and(block + group, 3) * 64

                def start_back(d, group=group, there=there):
                    p = jnp.bitwise_xor(member, jnp.bitwise_xor(d, FAR))
                    remote(
                        tile(b_send, p, 4),
                        tile(b_recv, column, 4),
                        b_send_sem.at[group],
                        b_recv_sem,
                        place(there + p),
                    ).start()
                    return 0

                if group:
                    lax.fori_loop(0, 64, lambda d, c: start_back(d), 0, unroll=4)
                else:
                    spread(start_back, 64, FAR)
            pltpu.make_async_copy(
                tile(b_send, member, 4), tile(b_recv, column, 4), b_recv_sem
            ).start()

        @pl.when(first_time)
        def _():
            wait_move(xck, xck_recv, 1)

        wait_rows(b_recv, 512, b_recv_sem)
        parts = [b_recv[pl.ds(r, N, stride=4), :] for r in range(4)]
        parts = mul_right(cat(parts, 0), small[R_BACK], small[R_BACK + 1])
        parts = cat([parts[r * N : (r + 1) * N] for r in range(4)], 1)
        parts = mul_left(small[R_OUT], small[R_OUT + 1], parts)
        for o in range(2):
            for f in range(2):
                rows = slice(f * H, (f + 1) * H)
                hartree = parts[rows, o * N : (o + 1) * N]
                density = parts[rows, (2 + o) * N : (3 + o) * N]
                cross = hartree + xck_recv[pl.ds(o * N + f, H, stride=2), :] * density
                cross_stage[pl.ds(o * N + f, H, stride=2), :] = cross
                base = (o * 4 + f * 2) * H
                cur[pl.ds(base, H), :] = other[o, f, 0] + step_time * cross * wave[o, f, 1]
                cur[pl.ds(base + H, H), :] = other[o, f, 1] - step_time * cross * wave[o, f, 0]

        @pl.when(owner)
        def _():
            wait_rows(h_send, 254, h_send_sem)
            wait_rows(b_send, 252, b_send_sem.at[0])
            for group in range(1, 4):
                wait_rows(b_send, 256, b_send_sem.at[group])

        @pl.when(jnp.logical_not(owner))
        def _():
            wait_rows(h_send, 256, h_send_sem)

    def pair(i, carry):
        sign = jnp.where(i < 4, 1.0, -1.0).astype(F32)
        columns(i, sign)
        start_inside(recv1, recv_sem.at[1])

        @pl.when(i == 0)
        def _():
            wait_rows(pot_recv, 256, move_recv.at[0])
            wait_rows(column_recv, 252, move_send.at[0])
            phase = phase_of(tile_values(pot_recv, 0.5 * SUB_TIME, 1, 2))
            write(plane_one, phase)
            write(plane_two, double(phase))


        wait_rows(recv1, 512, recv_sem.at[1])
        move_quarter(i, 1)
        wait_rows(send, 504, send_sem)
        turn = jnp.where(i < 4, AY, AY + 2)
        field = left(square[turn], square[turn + 1], read_tiles(recv1))

        @pl.when(i % 2 == 0)
        def _():
            write(cur, rotate(field, read(plane_two), sign))

        @pl.when(i % 2 == 1)
        def _():
            write(cur, rotate(field, read(plane_one), sign))

        @pl.when(i == 1)
        def _():
            psi_one[...] = cur[...]

        @pl.when(i == 3)
        def _():
            wait_move(cost, cost_recv, 2)
            psi[...] = cur[...]
            write(adj, read_planes(cost_recv))

        @pl.when(i == 5)
        def _():
            psi[...] = psi_one[...]
            adj[...] = cur[...]

        @pl.when(jnp.logical_or(i == 3, i == 5))
        def _():
            response(i == 3)

        sign_next = jnp.where(i < 3, 1.0, -1.0).astype(F32)

        @pl.when(i % 2 == 1)
        def _():
            write(cur, rotate(read(cur), read(plane_one), sign_next))

        turn = jnp.where(i < 3, AY, AY + 2)
        back = jnp.where(i < 3, BZ, BZ + 2)
        field = right(square[back], square[back + 1], read(cur))
        field = left(square[turn], square[turn + 1], field)
        write_tiles(send, field)

        @pl.when(jnp.logical_and(i == 0, jnp.logical_not(home)))
        def _():
            pl.semaphore_wait(known, 1)

        start_inside(recv0, recv_sem.at[0])
        return carry

    lax.fori_loop(0, 7, pair, 0)

    columns(jnp.int32(7), jnp.float32(-1.0))

    def start_last(d, carry):
        q = jnp.bitwise_xor(fft, jnp.bitwise_xor(d, FAR_PLANE))
        own = jnp.logical_and(home, d == FAR_PLANE)

        @pl.when(jnp.logical_not(own))
        def _():
            remote(
                tile(send, slot_of(q)), tile(recv_last, member), send_sem, last_sem, (point, q)
            ).start()

        @pl.when(own)
        def _():
            pltpu.make_async_copy(
                tile(send, slot_of(q)), tile(recv_last, member), last_sem
            ).start()

        return carry

    lax.fori_loop(0, 64, start_last, 0)

    pltpu.make_async_copy(cross_recv, cross_recv, move_recv.at[3]).wait()
    cross_out[...] = cross_recv[...]

    @pl.when(jnp.logical_not(stay))
    def _():
        pltpu.make_async_copy(cross_stage, cross_stage, move_send.at[3]).wait()

    wait_rows(recv_last, 512, last_sem)
    field = left(square[AY + 2], square[AY + 3], read_tiles(recv_last))
    field = rotate(field, read(orig_phase), -1.0)
    for o, f, c in PARTS:
        out[pl.ds((c * 2 + o) * N + f, H, stride=2), :] = field[o, f, c]

    @pl.when(home)
    def _():
        wait_rows(send, 504, send_sem)
        wait_rows(column_send, 252, phase_sem.at[0])

    @pl.when(jnp.logical_not(home))
    def _():
        wait_rows(send, 512, send_sem)
        wait_rows(column_send, 256, phase_sem.at[0])


def local(orbitals, costate, potential, xc_kernel, vector_potential, kpoint_weight, occupation):
    square, dft, small = constants()
    vmem = pl.BlockSpec(memory_space=pltpu.VMEM)
    smem = pl.BlockSpec(memory_space=pltpu.SMEM)
    hbm = pl.BlockSpec(memory_space=pltpu.HBM)

    def rows(count):
        return pltpu.VMEM((count, N), F32)

    field = rows(512)
    half = rows(256)
    dma = pltpu.SemaphoreType.DMA
    out, cross = pl.pallas_call(
        kernel,
        out_shape=(
            jax.ShapeDtypeStruct((512, N), F32),
            jax.ShapeDtypeStruct((256, N), F32),
        ),
        in_specs=[hbm] * 4 + [smem] * 3 + [hbm] * 3,
        out_specs=(vmem, vmem),
        scratch_shapes=[
            field, half, pltpu.VMEM(square.shape, BF), pltpu.VMEM(dft.shape, F32), pltpu.VMEM(small.shape, BF),
            field, field, field, field, half, half, field, half, half,
            field, field, field, field, field, field, field, field,
            pltpu.VMEM((2, 256, 256), BF), pltpu.VMEM((2, 256, 256), BF),
            rows(N), half, field, half, field, half, half,
            dma((5,)), dma, dma((2,)), dma, dma((2,)), dma((4,)), dma((4,)),
            dma, dma, dma((4,)), dma, pltpu.SemaphoreType.REGULAR,
        ],
        compiler_params=pltpu.CompilerParams(
            collective_id=0, has_side_effects=True, vmem_limit_bytes=60 * 1024 * 1024
        ),
        name="window",
    )(
        orbitals.reshape(512, N),
        costate.reshape(512, N),
        potential.reshape(256, N),
        xc_kernel.reshape(256, N),
        vector_potential,
        kpoint_weight,
        occupation,
        jnp.asarray(square),
        jnp.asarray(dft),
        jnp.asarray(small),
    )
    return out.reshape(orbitals.shape), cross.reshape(potential.shape)


def solution(mesh):
    placed = (
        P("ka", None, None, "fft", None, None),
        P("ka", None, None, "fft", None, None),
        P("fft", None, None),
        P("fft", None, None),
        P(),
        P(),
        P(),
    )
    return jax.shard_map(
        local,
        mesh=mesh,
        in_specs=placed,
        out_specs=(P("ka", None, None, "fft", None, None), P("fft", None, None)),
        check_vma=False,
    )
```

```python
import functools
import math

import jax
import jax.numpy as jnp
import ml_dtypes
import numpy as np
from jax import lax
from jax.experimental import pallas as pl
from jax.experimental.pallas import tpu as pltpu
from jax.sharding import PartitionSpec as P

MESH = pl.DeviceIdType.MESH
N = 128
H = 64
STEPS = 2
SUB = 4
FAR = 52
FAR_OWNER = 74
FAR_PLANE = 37
KPTS = 4
spacing = 0.25
step_time = 0.6
SUB_TIME = step_time / SUB
UNIT = 2.0 * math.pi / (N * spacing)
BF = jnp.bfloat16
F32 = jnp.float32
PARTS = [(o, f, c) for o in range(2) for f in range(2) for c in range(2)]


def swap(index):
    return (index % 2) * 2 + index // 2


def slot_of(pair):
    return (pair // 32) * 32 + ((pair // 2) % 4) * 8 + (pair % 2) * 4 + (pair // 8) % 4


def plane_of(slot):
    return (slot // 32) * 32 + (slot % 4) * 8 + ((slot // 8) % 4) * 2 + (slot // 4) % 2


def split(matrix):
    high = matrix.astype(np.float32).astype(ml_dtypes.bfloat16)
    low = (matrix - high.astype(np.float64)).astype(np.float32).astype(ml_dtypes.bfloat16)
    return high, low


def constants():
    line = np.arange(N)
    signed = np.where(line < H, line, line - N)
    forward = np.exp(-2j * np.pi / N * ((line[:, None] * line[None, :]) % N))
    inverse = forward.conj().T / N
    order = np.array([c * N + 2 * q + f for f in range(2) for c in range(2) for q in range(H)])
    slots = [plane_of(q) for q in range(H)]
    order_x = np.array([c * N + 2 * q + f for f in range(2) for c in range(2) for q in slots])

    def stacked(matrix):
        return np.block([[matrix.real, -matrix.imag], [matrix.imag, matrix.real]])

    square = []
    for shift, side in ((0.25, "left"), (-0.25, "right")):
        wave = UNIT * (shift + signed)
        for sign in (1.0, -1.0):
            phase = np.exp(-1j * sign * 0.5 * SUB_TIME * wave * wave)
            full = stacked(inverse @ (phase[:, None] * forward))
            full = full[order][:, order] if side == "left" else full.T
            square += list(split(full))
    square += list(split(stacked(inverse)[order_x]))
    dft = stacked(forward)[:, order_x].astype(np.float32)

    real = np.zeros((N, N))
    real[0] = 1.0 / math.sqrt(N)
    real[N - 1] = np.cos(np.pi * line) / math.sqrt(N)
    for k in range(1, H):
        real[2 * k - 1] = math.sqrt(2.0 / N) * np.cos(2.0 * np.pi * (k * line % N) / N)
        real[2 * k] = math.sqrt(2.0 / N) * np.sin(2.0 * np.pi * (k * line % N) / N)
    pairs = np.array([2 * q + f for f in range(2) for q in range(H)])
    pairs_x = np.array([2 * q + f for f in range(2) for q in slots])
    small = []
    for matrix in (
        real[:, pairs], real[:, pairs].T, real.T, real, real[:, pairs_x], real[:, pairs_x].T,
    ):
        small += list(split(matrix))
    return np.stack(square), dft, np.stack(small)


AY, BZ, FINV = 0, 4, 8
R_IN, R_OUT, R_RIGHT, R_BACK, X_IN, X_OUT = 0, 2, 4, 6, 8, 10


def halves(value):
    high = value.astype(BF)
    return high, (value - high.astype(F32)).astype(BF)


def dot(a, b):
    return jnp.dot(a, b, preferred_element_type=F32)


def mul_left(high, low, value):
    vh, vl = halves(value)
    return dot(high, vh) + (dot(high, vl) + dot(low, vh))


def mul_right(value, high, low):
    vh, vl = halves(value)
    return dot(vh, high) + (dot(vl, high) + dot(vh, low))


def cat(values, axis):
    return jnp.concatenate(values, axis=axis)


def left(high, low, field):
    rows = [cat([field[0, f, c], field[1, f, c]], 1) for f in range(2) for c in range(2)]
    out = mul_left(high, low, cat(rows, 0))
    return {
        (o, f, c): out[(f * 2 + c) * H : (f * 2 + c + 1) * H, o * N : (o + 1) * N]
        for o, f, c in PARTS
    }


def right(high, low, field):
    rows = [cat([field[o, f, 0], field[o, f, 1]], 1) for o in range(2) for f in range(2)]
    out = mul_right(cat(rows, 0), high, low)
    return {
        (o, f, c): out[(o * 2 + f) * H : (o * 2 + f + 1) * H, c * N : (c + 1) * N]
        for o, f, c in PARTS
    }


def rotate(field, phase, sign):
    out = {}
    for o in range(2):
        for f in range(2):
            cosine, sine = phase[o, f, 0], sign * phase[o, f, 1]
            re, im = field[o, f, 0], field[o, f, 1]
            out[o, f, 0] = re * cosine + im * sine
            out[o, f, 1] = im * cosine - re * sine
    return out


def double(phase):
    out = {}
    for o in range(2):
        for f in range(2):
            cosine, sine = phase[o, f, 0], phase[o, f, 1]
            out[o, f, 0] = cosine * cosine - sine * sine
            out[o, f, 1] = 2.0 * cosine * sine
    return out


def read(ref):
    return {(o, f, c): ref[pl.ds((o * 4 + f * 2 + c) * H, H), :] for o, f, c in PARTS}


def write(ref, field):
    for o, f, c in PARTS:
        ref[pl.ds((o * 4 + f * 2 + c) * H, H), :] = field[o, f, c]


def read_tiles(ref):
    return {(o, f, c): ref[pl.ds(o * 4 + f * 2 + c, H, stride=8), :] for o, f, c in PARTS}


def write_tiles(ref, field):
    for o, f, c in PARTS:
        ref[pl.ds(f * 4 + o * 2 + c, H, stride=8), :] = field[o, f, c]


def read_planes(ref):
    return {(o, f, c): ref[pl.ds((c * 2 + o) * N + f, H, stride=2), :] for o, f, c in PARTS}


def phase_of(angles):
    out = {}
    for (o, f), angle in angles.items():
        out[o, f, 0] = jnp.cos(angle)
        out[o, f, 1] = jnp.sin(angle)
    return out


def plane_values(ref, factor):
    return {
        (o, f): factor * ref[pl.ds(o * N + f, H, stride=2), :] for o in range(2) for f in range(2)
    }


def tile_values(ref, factor, step_own, step_far):
    return {
        (o, f): factor * ref[pl.ds(o * step_own + f * step_far, H, stride=4), :]
        for o in range(2)
        for f in range(2)
    }


def kernel(
    orb_in, cost, pot_in, xck, vec, weight, occupation, square_in, dft_in, small_in,
    out, cross_out,
    orb, pot, square, dft, small,
    send, recv0, recv1, recv_last, column_send, column_recv, cost_recv, pot_recv, xck_recv,
    orig_phase, plane_one, plane_two, col_two, cur, psi_one, psi, adj, first, second,
    coulomb, h_send, h_recv, b_send, b_recv, cross_stage, cross_recv,
    load_sem, send_sem, recv_sem, last_sem, phase_sem, move_send, move_recv,
    h_send_sem, h_recv_sem, b_send_sem, b_recv_sem, known,
):
    ka = lax.axis_index("ka")
    fft = lax.axis_index("fft")
    block = fft // 16
    member = (fft % 16) * 4 + ka
    ident = fft * 4 + ka
    point = swap(block)
    goal = swap(ka)
    home = block == goal
    slot = slot_of(fft)
    plane = plane_of(member)
    stay = jnp.logical_and(home, member == slot)

    def place(p):
        return (jnp.bitwise_and(p, 3), lax.shift_right_logical(p, 2))

    def spread(start, count, own, unroll=4):
        lax.fori_loop(0, own, lambda d, c: start(d), 0, unroll=unroll)
        lax.fori_loop(own + 1, count, lambda d, c: start(d), 0, unroll=count - own - 1)

    def remote(src, dst, ss, rs, device):
        return pltpu.make_async_remote_copy(
            src_ref=src, dst_ref=dst, send_sem=ss, recv_sem=rs, device_id=device, device_id_type=MESH
        )

    def wait_rows(ref, rows, sem):
        part = ref.at[pl.ds(0, rows)]
        pltpu.make_async_copy(part, part, sem).wait()

    def tile(ref, index, rows=8):
        return ref.at[pl.ds(pl.multiple_of(index * rows, rows), rows)]

    loads = [
        pltpu.make_async_copy(src, dst, load_sem.at[index])
        for index, (src, dst) in enumerate(
            ((pot_in, pot), (orb_in, orb), (square_in, square), (dft_in, dft), (small_in, small))
        )
    ]
    for load in loads:
        load.start()

    barrier = pltpu.get_barrier_semaphore()

    def greet(d, carry):
        peer = jnp.bitwise_xor(fft, d)

        @pl.when(jnp.logical_not(jnp.logical_and(home, d == 0)))
        def _():
            pl.semaphore_signal(barrier, inc=1, device_id=(point, peer), device_id_type=MESH)

        return carry

    lax.fori_loop(0, 64, greet, 0)

    loads[0].wait()
    for o in range(2):
        for f in range(2):
            column_send[pl.ds(f * 2 + o, H, stride=4), :] = pot[pl.ds(o * N + f, H, stride=2), :]
    phase = phase_of(plane_values(pot, 0.5 * SUB_TIME))
    write(orig_phase, phase)
    loads[1].wait()
    field = rotate(read_planes(orb), phase, 1.0)
    loads[2].wait()
    field = right(square[BZ], square[BZ + 1], field)
    field = left(square[AY], square[AY + 1], field)
    write_tiles(send, field)

    @pl.when(home)
    def _():
        pl.semaphore_wait(barrier, 63)

    @pl.when(jnp.logical_not(home))
    def _():
        pl.semaphore_wait(barrier, 64)

    def start_first(src, dst, rows, ss, rs):
        def start(d, carry):
            p = jnp.bitwise_xor(member, jnp.bitwise_xor(d, FAR))
            own = jnp.logical_and(home, d == FAR)

            @pl.when(jnp.logical_not(own))
            def _():
                device = place(goal * 64 + p)
                remote(tile(src, p, rows), tile(dst, slot, rows), ss, rs, device).start()

            @pl.when(own)
            def _():
                pltpu.make_async_copy(tile(src, p, rows), tile(dst, slot, rows), rs).start()

            return carry

        lax.fori_loop(0, 64, start, 0)

    start_first(send, recv0, 8, send_sem, recv_sem.at[0])
    start_first(column_send, column_recv, 4, phase_sem.at[0], phase_sem.at[1])

    def start_move(src, dst, index):
        @pl.when(stay)
        def _():
            pltpu.make_async_copy(src, dst, move_recv.at[index]).start()

        @pl.when(jnp.logical_not(stay))
        def _():
            device = place(goal * 64 + slot)
            remote(src, dst, move_send.at[index], move_recv.at[index], device).start()

    def wait_move(src, dst, index):
        pltpu.make_async_copy(dst, dst, move_recv.at[index]).wait()

        @pl.when(jnp.logical_not(stay))
        def _():
            pltpu.make_async_copy(src, src, move_send.at[index]).wait()

    column = fft * 2 + ka // 2
    owner = ka % 2 == 0
    unit_y = (UNIT * ((column + 1) // 2)).astype(F32)
    along_x = (lax.broadcasted_iota(jnp.int32, (N, N), 0) + 1) // 2
    along_z = (lax.broadcasted_iota(jnp.int32, (N, N), 1) + 1) // 2
    wave_x = UNIT * along_x.astype(F32)
    wave_z = UNIT * along_z.astype(F32)
    g_squared = wave_x * wave_x + unit_y * unit_y + wave_z * wave_z
    positive = g_squared > 0
    coulomb[...] = jnp.where(positive, 4.0 * math.pi / jnp.where(positive, g_squared, 1.0), 0.0)

    shift_x = UNIT * ((point.astype(F32) + 0.5) / KPTS - 0.5)

    def build(target, sub_index, sign):
        mode = lax.broadcasted_iota(jnp.int32, (N, N), 0)
        mode = jnp.where(mode < H, mode, mode - N).astype(F32)
        wave = shift_x + UNIT * mode + vec[sub_index]
        angle = (0.5 * SUB_TIME) * (wave * wave)
        cosine, sine = jnp.cos(angle), sign * jnp.sin(angle)
        cosine, sine = cat([cosine, cosine], 1), cat([sine, sine], 1)
        re, im = dft[0:N, :], dft[N : 2 * N, :]
        turned = cat([re * cosine + im * sine, im * cosine - re * sine], 0)
        made = mul_left(square[FINV], square[FINV + 1], turned)
        high, low = halves(made)
        target[0] = high
        target[1] = low

    def start_inside(target, sem):
        def start(d):
            p = jnp.bitwise_xor(member, jnp.bitwise_xor(d, FAR))
            remote(
                tile(send, p), tile(target, member), send_sem, sem, place(block * 64 + p)
            ).start()
            return 0

        spread(start, 64, FAR)
        pltpu.make_async_copy(tile(send, member), tile(target, member), sem).start()

    def move_quarter(i, part):
        @pl.when(jnp.logical_or(i == 1, i == 2))
        def _():
            quarter = 2 * (i - 1) + part
            start_move(tile(cost, quarter, N), tile(cost_recv, quarter, N), 2)

        @pl.when(i == 3 - 3 * part)
        def _():
            start_move(tile(xck, 1 - part, N), tile(xck_recv, 1 - part, N), 1)

        @pl.when(i == 6)
        def _():
            src, dst = tile(cross_stage, part, N), tile(cross_recv, part, N)

            @pl.when(stay)
            def _():
                pltpu.make_async_copy(src, dst, move_recv.at[3]).start()

            @pl.when(jnp.logical_not(stay))
            def _():
                remote(src, dst, move_send.at[3], move_recv.at[3], (point, plane)).start()

    def columns(i, sign):
        forward = i < 4

        @pl.when(i == 0)
        def _():
            loads[3].wait()
            loads[4].wait()

        build(first, jnp.where(forward, 2 * i, 15 - 2 * i), sign)
        build(second, jnp.where(forward, 2 * i + 1, 14 - 2 * i), sign)
        wait_rows(recv0, 512, recv_sem.at[0])
        move_quarter(i, 0)

        @pl.when(jnp.logical_and(i == 0, jnp.logical_not(home)))
        def _():
            wait_rows(send, 512, send_sem)

        @pl.when(jnp.logical_or(i > 0, home))
        def _():
            wait_rows(send, 504, send_sem)

        field = left(first[0], first[1], read_tiles(recv0))

        @pl.when(i == 0)
        def _():
            wait_rows(column_recv, 256, phase_sem.at[1])

            def start_planes(d):
                p = jnp.bitwise_xor(member, jnp.bitwise_xor(d, FAR))
                remote(
                    tile(column_recv, p, 4),
                    tile(pot_recv, member, 4),
                    move_send.at[0],
                    move_recv.at[0],
                    place(block * 64 + p),
                ).start()
                return 0

            spread(start_planes, 64, FAR)
            pltpu.make_async_copy(
                tile(column_recv, member, 4), tile(pot_recv, member, 4), move_recv.at[0]
            ).start()
            write(col_two, phase_of(tile_values(column_recv, SUB_TIME, 2, 1)))

            @pl.when(ka == 0)
            def _():
                for step in range(1, 4):
                    other = (block + step) % 4
                    pl.semaphore_signal(
                        known, inc=1, device_id=(point, other * 16 + fft % 16), device_id_type=MESH
                    )

        field = rotate(field, read(col_two), sign)
        field = left(second[0], second[1], field)
        back = jnp.where(forward, BZ, BZ + 2)
        field = right(square[back], square[back + 1], field)
        write_tiles(send, field)

    def response(first_time):
        wave, other = read(psi), read(adj)
        total = weight[0] + weight[1] + weight[2] + weight[3]
        share = weight[point].astype(F32) / total.astype(F32)
        factor = 2.0 * share * (occupation[0].astype(F32) / 100.0)
        own = {
            (o, f): factor * (other[o, f, 0] * wave[o, f, 0] + other[o, f, 1] * wave[o, f, 1])
            for o in range(2)
            for f in range(2)
        }
        dense = cat([cat([own[0, f], own[1, f]], 1) for f in range(2)], 0)
        dense = mul_left(small[R_IN], small[R_IN + 1], dense)
        dense = mul_right(
            cat([dense[:, 0:N], dense[:, N : 2 * N]], 0), small[R_RIGHT], small[R_RIGHT + 1]
        )
        for o in range(2):
            h_send[pl.ds(o, N, stride=2), :] = dense[o * N : (o + 1) * N]

        def send_dense(to):
            device = (jnp.bitwise_and(to, 1) * 2, lax.shift_right_logical(to, 1))
            remote(
                tile(h_send, to, 2), tile(h_recv, ident, 2), h_send_sem, h_recv_sem, device
            ).start()

        def start_dense(d):
            send_dense(jnp.bitwise_xor(column, jnp.bitwise_xor(d, FAR_OWNER)))
            return 0

        lax.fori_loop(0, FAR_OWNER, lambda d, c: start_dense(d), 0, unroll=2)
        lax.fori_loop(FAR_OWNER + 1, N, lambda d, c: start_dense(d), 0)

        @pl.when(owner)
        def _():
            pltpu.make_async_copy(
                tile(h_send, column, 2), tile(h_recv, ident, 2), h_recv_sem
            ).start()

        @pl.when(jnp.logical_not(owner))
        def _():
            send_dense(column)

        @pl.when(owner)
        def _():
            wait_rows(h_recv, 512, h_recv_sem)
            summed = []
            for f in range(2):
                terms = [h_recv[pl.ds(k * N + f, H, stride=2), :] for k in range(4)]
                summed.append((terms[0] + terms[1]) + (terms[2] + terms[3]))
            line = mul_left(small[X_IN], small[X_IN + 1], cat(summed, 0)) * coulomb[...]
            line = mul_left(small[X_OUT], small[X_OUT + 1], line)
            for f in range(2):
                b_send[pl.ds(f, H, stride=4), :] = line[f * H : (f + 1) * H]
                b_send[pl.ds(2 + f, H, stride=4), :] = summed[f]
            for group in (2, 3, 1, 0):
                there = jnp.bitwise_and(block + group, 3) * 64

                def start_back(d, group=group, there=there):
                    p = jnp.bitwise_xor(member, jnp.bitwise_xor(d, FAR))
                    remote(
                        tile(b_send, p, 4),
                        tile(b_recv, column, 4),
                        b_send_sem.at[group],
                        b_recv_sem,
                        place(there + p),
                    ).start()
                    return 0

                if group:
                    lax.fori_loop(0, 64, lambda d, c: start_back(d), 0, unroll=4)
                else:
                    spread(start_back, 64, FAR)
            pltpu.make_async_copy(
                tile(b_send, member, 4), tile(b_recv, column, 4), b_recv_sem
            ).start()

        @pl.when(first_time)
        def _():
            wait_move(xck, xck_recv, 1)

        wait_rows(b_recv, 512, b_recv_sem)
        parts = [b_recv[pl.ds(r, N, stride=4), :] for r in range(4)]
        parts = mul_right(cat(parts, 0), small[R_BACK], small[R_BACK + 1])
        parts = cat([parts[r * N : (r + 1) * N] for r in range(4)], 1)
        parts = mul_left(small[R_OUT], small[R_OUT + 1], parts)
        for o in range(2):
            for f in range(2):
                rows = slice(f * H, (f + 1) * H)
                hartree = parts[rows, o * N : (o + 1) * N]
                density = parts[rows, (2 + o) * N : (3 + o) * N]
                cross = hartree + xck_recv[pl.ds(o * N + f, H, stride=2), :] * density
                cross_stage[pl.ds(o * N + f, H, stride=2), :] = cross
                base = (o * 4 + f * 2) * H
                cur[pl.ds(base, H), :] = other[o, f, 0] + step_time * cross * wave[o, f, 1]
                cur[pl.ds(base + H, H), :] = other[o, f, 1] - step_time * cross * wave[o, f, 0]

        @pl.when(owner)
        def _():
            wait_rows(h_send, 254, h_send_sem)
            wait_rows(b_send, 252, b_send_sem.at[0])
            for group in range(1, 4):
                wait_rows(b_send, 256, b_send_sem.at[group])

        @pl.when(jnp.logical_not(owner))
        def _():
            wait_rows(h_send, 256, h_send_sem)

    def pair(i, carry):
        sign = jnp.where(i < 4, 1.0, -1.0).astype(F32)
        columns(i, sign)
        start_inside(recv1, recv_sem.at[1])

        @pl.when(i == 0)
        def _():
            wait_rows(pot_recv, 256, move_recv.at[0])
            wait_rows(column_recv, 252, move_send.at[0])
            phase = phase_of(tile_values(pot_recv, 0.5 * SUB_TIME, 1, 2))
            write(plane_one, phase)
            write(plane_two, double(phase))


        wait_rows(recv1, 512, recv_sem.at[1])
        move_quarter(i, 1)
        wait_rows(send, 504, send_sem)
        turn = jnp.where(i < 4, AY, AY + 2)
        field = left(square[turn], square[turn + 1], read_tiles(recv1))

        @pl.when(i % 2 == 0)
        def _():
            write(cur, rotate(field, read(plane_two), sign))

        @pl.when(i % 2 == 1)
        def _():
            write(cur, rotate(field, read(plane_one), sign))

        @pl.when(i == 1)
        def _():
            psi_one[...] = cur[...]

        @pl.when(i == 3)
        def _():
            wait_move(cost, cost_recv, 2)
            psi[...] = cur[...]
            write(adj, read_planes(cost_recv))

        @pl.when(i == 5)
        def _():
            psi[...] = psi_one[...]
            adj[...] = cur[...]

        @pl.when(jnp.logical_or(i == 3, i == 5))
        def _():
            response(i == 3)

        sign_next = jnp.where(i < 3, 1.0, -1.0).astype(F32)

        @pl.when(i % 2 == 1)
        def _():
            write(cur, rotate(read(cur), read(plane_one), sign_next))

        turn = jnp.where(i < 3, AY, AY + 2)
        back = jnp.where(i < 3, BZ, BZ + 2)
        field = right(square[back], square[back + 1], read(cur))
        field = left(square[turn], square[turn + 1], field)
        write_tiles(send, field)

        @pl.when(jnp.logical_and(i == 0, jnp.logical_not(home)))
        def _():
            pl.semaphore_wait(known, 1)

        start_inside(recv0, recv_sem.at[0])
        return carry

    lax.fori_loop(0, 7, pair, 0)

    columns(jnp.int32(7), jnp.float32(-1.0))

    def start_last(d, carry):
        q = jnp.bitwise_xor(fft, jnp.bitwise_xor(d, FAR_PLANE))
        own = jnp.logical_and(home, d == FAR_PLANE)

        @pl.when(jnp.logical_not(own))
        def _():
            remote(
                tile(send, slot_of(q)), tile(recv_last, member), send_sem, last_sem, (point, q)
            ).start()

        @pl.when(own)
        def _():
            pltpu.make_async_copy(
                tile(send, slot_of(q)), tile(recv_last, member), last_sem
            ).start()

        return carry

    lax.fori_loop(0, 64, start_last, 0)

    pltpu.make_async_copy(cross_recv, cross_recv, move_recv.at[3]).wait()
    cross_out[...] = cross_recv[...]

    @pl.when(jnp.logical_not(stay))
    def _():
        pltpu.make_async_copy(cross_stage, cross_stage, move_send.at[3]).wait()

    wait_rows(recv_last, 512, last_sem)
    field = left(square[AY + 2], square[AY + 3], read_tiles(recv_last))
    field = rotate(field, read(orig_phase), -1.0)
    for o, f, c in PARTS:
        out[pl.ds((c * 2 + o) * N + f, H, stride=2), :] = field[o, f, c]

    @pl.when(home)
    def _():
        wait_rows(send, 504, send_sem)
        wait_rows(column_send, 252, phase_sem.at[0])

    @pl.when(jnp.logical_not(home))
    def _():
        wait_rows(send, 512, send_sem)
        wait_rows(column_send, 256, phase_sem.at[0])


def local(orbitals, costate, potential, xc_kernel, vector_potential, kpoint_weight, occupation):
    square, dft, small = constants()
    vmem = pl.BlockSpec(memory_space=pltpu.VMEM)
    smem = pl.BlockSpec(memory_space=pltpu.SMEM)
    hbm = pl.BlockSpec(memory_space=pltpu.HBM)

    def rows(count):
        return pltpu.VMEM((count, N), F32)

    field = rows(512)
    half = rows(256)
    dma = pltpu.SemaphoreType.DMA
    out, cross = pl.pallas_call(
        kernel,
        out_shape=(
            jax.ShapeDtypeStruct((512, N), F32),
            jax.ShapeDtypeStruct((256, N), F32),
        ),
        in_specs=[hbm] * 4 + [smem] * 3 + [hbm] * 3,
        out_specs=(vmem, vmem),
        scratch_shapes=[
            field, half, pltpu.VMEM(square.shape, BF), pltpu.VMEM(dft.shape, F32), pltpu.VMEM(small.shape, BF),
            field, field, field, field, half, half, field, half, half,
            field, field, field, field, field, field, field, field,
            pltpu.VMEM((2, 256, 256), BF), pltpu.VMEM((2, 256, 256), BF),
            rows(N), half, field, half, field, half, half,
            dma((5,)), dma, dma((2,)), dma, dma((2,)), dma((4,)), dma((4,)),
            dma, dma, dma((4,)), dma, pltpu.SemaphoreType.REGULAR,
        ],
        compiler_params=pltpu.CompilerParams(
            collective_id=0, has_side_effects=True, vmem_limit_bytes=60 * 1024 * 1024
        ),
        name="window",
    )(
        orbitals.reshape(512, N),
        costate.reshape(512, N),
        potential.reshape(256, N),
        xc_kernel.reshape(256, N),
        vector_potential,
        kpoint_weight,
        occupation,
        jnp.asarray(square),
        jnp.asarray(dft),
        jnp.asarray(small),
    )
    return out.reshape(orbitals.shape), cross.reshape(potential.shape)


def solution(mesh):
    placed = (
        P("ka", None, None, "fft", None, None),
        P("ka", None, None, "fft", None, None),
        P("fft", None, None),
        P("fft", None, None),
        P(),
        P(),
        P(),
    )
    return jax.shard_map(
        local,
        mesh=mesh,
        in_specs=placed,
        out_specs=(P("ka", None, None, "fft", None, None), P("fft", None, None)),
        check_vma=False,
    )
```
